256 devices in a mesh: seq: 32 (over z, y), tp: 8 (over x, core).
Axes of the slice: x: 4, y: 4, z: 8, core: 2. Of those that a mesh axis runs over, the one named last changes fastest.
Arguments:
- tokens: bfloat16 [16384, 4096], P('seq'), may hold values from -80 to 80
- norm_gain: float32 [4096], replicated, may hold values from 0.1 to 1.9
- query_weight: bfloat16 [4096, 4096], P(None, 'tp'), may hold values from -1 to 1
- key_weight: bfloat16 [4096, 1024], P(None, 'tp'), may hold values from -8 to 8
- value_weight: bfloat16 [4096, 1024], P(None, 'tp'), may hold values from -0.09375 to 0.09375
- out_weight: bfloat16 [4096, 4096], P(None, 'tp'), may hold values from -1 to 1
- segments: int32 [16384], replicated, may hold values from 0 to 2, never falling along the last dimension, each value on 1 to 8192 neighbouring positions
Outputs:
- attn_out: bfloat16 [16384, 4096], P('seq', 'tp')
The draws below stay inside these ranges and needn't reach their ends.
All inputs are finite; a program needn't handle non-finite values.
Results may differ from the reference program's by a relative error of at most 0.013.
The reference program's roundings to bfloat16 on the way (of `normed`, `queries`, `keys`, `values`, `probabilities` and `attended`) count: a program that leaves them out, or rounds other values in their place, can miss the bound.
Values may be sent and summed in bfloat16 or wider, within the bound.
A program may use at most 128 MiB of HBM per device.

```python
import math
import jax
import jax.numpy as jnp
import numpy as np
from jax import lax

D = 4096
HEADS = 32
KV_HEADS = 8
HEAD_DIM = 128
WINDOW = 4096
TOK_DEV = 512
TOKENS = 16384
HALO = 8
N_SEQ = 32


def shared_query(key):
    return jax.random.normal(jax.random.fold_in(key, 11), (D, HEADS * HEAD_DIM), jnp.float32) / math.sqrt(D)


def draw_query_weight(key, part):
    return jnp.clip(shared_query(key), -1.0, 1.0).astype(jnp.bfloat16)


def draw_key_weight(key, part):
    base = jax.random.normal(jax.random.fold_in(key, 13), (D, KV_HEADS * HEAD_DIM), jnp.float32) / math.sqrt(D)
    return jnp.clip(base, -8.0, 8.0).astype(jnp.bfloat16)


def draw_tokens(key, part):
    base = jax.random.normal(jax.random.fold_in(key, 17), (TOKENS, D), jnp.float32)
    base = jnp.clip(base, -6.0, 6.0)
    return base.astype(jnp.bfloat16)


def block_levels(rng, extent, split, low, largest):
    def one(position, blocks):
        steps = jax.random.uniform(jax.random.fold_in(jax.random.fold_in(rng, 6), position), (blocks,), jnp.float32, low / len(split), largest / len(split))
        return jnp.repeat(jnp.exp(steps), extent[position] // blocks).reshape((-1,) + (1,) * (len(extent) - position - 1))

    factor_of = one(*split[0])
    for cut in split[1:]:
        factor_of = factor_of * one(*cut)
    return factor_of


def split_up(number_of, total, most, lean):
    weights = [(1 << 20) // math.isqrt(rank ** lean) + 1 for rank in range(2, number_of + 1)]
    surplus, counts = total - most - (number_of - 1), [1] * (number_of - 1)
    while surplus > 0:
        candidates = [i for i in range(number_of - 1) if counts[i] < most]
        mass, budget = sum([weights[i] for i in candidates]), surplus
        for i in candidates:
            extra = min(most - counts[i], max(1, budget * weights[i] // mass), surplus)
            counts[i] = counts[i] + extra
            surplus = surplus - extra
    return np.array([most] + counts)


def ragged_sizes(stream_key, count, total, most, skew):
    if count == 2:
        one = jax.random.randint(stream_key, (), max(1, total - most), min(most, total - 1) + 1)
        return jnp.stack([one, total - one])
    sizes = jnp.asarray(split_up(count, total, most, skew), jnp.int32)
    couples = (count - 1) // 2
    donor, taker = sizes[1:1 + 2 * couples:2], sizes[2:2 + 2 * couples:2]
    margin = jnp.minimum(donor - 1, most - taker)
    shifted = jax.random.randint(jax.random.fold_in(stream_key, 1), (couples,), 0, 1 << 20) % (margin + 1)
    sizes = sizes.at[1:1 + 2 * couples:2].set(donor - shifted).at[2:2 + 2 * couples:2].set(taker + shifted)
    return sizes[jax.random.permutation(jax.random.fold_in(stream_key, 2), count)]


def normal_values(rng, dims, scale, most, cuts=(), held_as=jnp.bfloat16):
    drawn = scale * jax.random.normal(rng, dims, jnp.float32)
    if cuts:
        drawn = drawn * block_levels(rng, dims, cuts, -0.22, 0.18)
    return jnp.clip(drawn, -most, most).astype(held_as)


def setup_inputs(seed: int = 0) -> dict:
    splits = jax.random.split(jax.random.key(seed), 8)
    tokens = draw_tokens(jax.random.fold_in(splits[7], 71), 0)
    norm_gain = jnp.clip(1.0 + 0.18 * jax.random.normal(splits[1], (D,), jnp.float32), 0.1, 1.9)
    query_weight = draw_query_weight(jax.random.fold_in(splits[7], 71), 0)
    key_weight = draw_key_weight(jax.random.fold_in(splits[7], 71), 0)
    value_weight = normal_values(splits[4], (D, KV_HEADS * HEAD_DIM), D ** -0.5, 0.09375, ((1, 8),))
    out_weight = normal_values(splits[5], (HEADS * HEAD_DIM, D), (HEAD_DIM // 4) ** -0.5, 1.0, ((1, 8),))
    segments = jnp.searchsorted(jnp.cumsum(ragged_sizes(splits[6], 3, TOKENS, TOKENS // 2, 0)), jnp.arange(TOKENS), side="right").astype(jnp.int32)
    return {"tokens": tokens, "norm_gain": norm_gain, "query_weight": query_weight, "key_weight": key_weight, "value_weight": value_weight, "out_weight": out_weight, "segments": segments}


def rotate(vectors, positions):
    half_dim = vectors.shape[-1] // 2
    freqs = 10000.0 ** (-(jnp.arange(half_dim, dtype=jnp.float32) * 2.0 / vectors.shape[-1]))
    angles = positions[:, None] * freqs[None, :]
    cosine = jnp.cos(angles)[:, None, :]
    sine_part = jnp.sin(angles)[:, None, :]
    first = vectors[..., :half_dim]
    second = vectors[..., half_dim:]
    return jnp.concatenate([first * cosine - second * sine_part, second * cosine + first * sine_part], axis=-1)

def project(normed, weight, positions):
    product = jnp.dot(normed, weight, preferred_element_type=jnp.float32)
    shaped = product.reshape(product.shape[0], -1, HEAD_DIM)
    return rotate(shaped, positions).astype(jnp.bfloat16)

def attend(queries, keys, values, allowed):
    block_rows, query_heads, head_size = queries.shape
    value_heads = keys.shape[1]
    grouped = queries.astype(jnp.float32).reshape(block_rows, value_heads, query_heads // value_heads, head_size)
    scores = jnp.einsum('tkgd,skd->kgts', grouped, keys.astype(jnp.float32)) / math.sqrt(head_size)
    scores = jnp.where(allowed[None, None], scores, jnp.float32(-1e+30))
    peak = lax.optimization_barrier(jnp.max(scores, axis=-1, keepdims=True))
    weights = jnp.exp(scores - peak)
    totals = lax.optimization_barrier(jnp.sum(weights, axis=-1, keepdims=True))
    probabilities = (weights / totals).astype(jnp.bfloat16)
    attended = jnp.einsum('kgts,skd->tkgd', probabilities.astype(jnp.float32), values.astype(jnp.float32))
    return attended.reshape(block_rows, query_heads * head_size).astype(jnp.bfloat16)

def reference(tokens, norm_gain, query_weight, key_weight, value_weight, out_weight, segments):
    widened = tokens.astype(jnp.float32)
    scale = lax.rsqrt(lax.optimization_barrier(jnp.mean(widened * widened, axis=-1, keepdims=True)) + 1e-05)
    normed = (widened * scale * norm_gain[None, :]).astype(jnp.bfloat16)
    positions = jnp.arange(TOKENS, dtype=jnp.int32).astype(jnp.float32)
    queries = project(normed, query_weight, positions)
    keys = project(normed, key_weight, positions)
    values = jnp.dot(normed, value_weight, preferred_element_type=jnp.float32).astype(jnp.bfloat16)
    values = values.reshape(TOKENS, KV_HEADS, HEAD_DIM)
    front = HALO * TOK_DEV
    span = (HALO + 1) * TOK_DEV
    padded_keys = jnp.concatenate([jnp.zeros((front, KV_HEADS, HEAD_DIM), jnp.bfloat16), keys], axis=0)
    padded_values = jnp.concatenate([jnp.zeros((front, KV_HEADS, HEAD_DIM), jnp.bfloat16), values], axis=0)
    padded_segments = jnp.concatenate([jnp.full((front,), -1, jnp.int32), segments.astype(jnp.int32)], axis=0)

    def one_block(block):
        start = (block * TOK_DEV).astype(jnp.int32)
        query_block = lax.dynamic_slice_in_dim(queries, start, TOK_DEV, 0)
        key_block = lax.dynamic_slice_in_dim(padded_keys, start, span, 0)
        value_block = lax.dynamic_slice_in_dim(padded_values, start, span, 0)
        query_segments = lax.dynamic_slice_in_dim(segments.astype(jnp.int32), start, TOK_DEV, 0)
        key_segments = lax.dynamic_slice_in_dim(padded_segments, start, span, 0)
        query_pos = start + jnp.arange(TOK_DEV, dtype=jnp.int32)
        key_pos = start - front + jnp.arange(span, dtype=jnp.int32)
        distance = query_pos[:, None] - key_pos[None, :]
        allowed = (distance >= 0) & (distance < WINDOW) & (key_segments[None, :] == query_segments[:, None])
        return attend(query_block, key_block, value_block, allowed)
    attended = lax.map(one_block, jnp.arange(N_SEQ, dtype=jnp.int32)).reshape(TOKENS, HEADS * HEAD_DIM)
    return jnp.dot(attended, out_weight, preferred_element_type=jnp.float32).astype(jnp.bfloat16)
```

```python
import math

import jax
import jax.numpy as jnp
from jax import lax
from jax.experimental import pallas as pl
from jax.experimental.pallas import tpu as pltpu
from jax.sharding import PartitionSpec as P

HEAD_DIM = 128
WINDOW = 4096
TILES = 4
NB = 3
Z1, Z2, LA, L1, RA, R1, LX, RX = range(1, 9)
F32 = jnp.float32
BF16 = jnp.bfloat16


def pick(y, options):
    value = jnp.int32(options[3])
    for i in (2, 1, 0):
        value = jnp.where(y == i, jnp.int32(options[i]), value)
    return value


def kernel(tok_hbm, gain_ref, cos_ref, sin_ref, lo_ref, wq_hbm, wk_hbm, wv_hbm, wo_hbm, out_ref,
           xs, nrm, wq, wkv, wo, kv, qs, m_s, acc, gb,
           tok_sem, w_sem, ksend, krecv, gsend, grecv):
    rows, width = xs.shape
    heads = wq.shape[1] // HEAD_DIM
    tile = rows // TILES
    seq = lax.axis_index("seq")
    tp = lax.axis_index("tp")
    y = lax.rem(seq, 4)
    z = seq // 4
    row0 = z * 4
    z_next = lax.rem(seq + 4, 32)
    z_prev = lax.rem(seq + 28, 32)
    right = row0 + lax.rem(y + 1, 4)
    left = row0 + lax.rem(y + 3, 4)
    core = lax.rem(tp, 2)
    x_right = lax.rem(tp + 2, 8)
    x_left = lax.rem(tp + 6, 8)
    sib = tp + 1 - 2 * core
    opposite = lax.rem(tp + 4, 8)

    tok_copies = [
        pltpu.make_async_copy(tok_hbm.at[pl.ds(i * tile, tile)], xs.at[pl.ds(i * tile, tile)], tok_sem.at[i])
        for i in range(TILES)
    ]
    wk_copy = pltpu.make_async_copy(wk_hbm, wkv.at[:, pl.ds(0, HEAD_DIM)], w_sem.at[0])
    wv_copy = pltpu.make_async_copy(wv_hbm, wkv.at[:, pl.ds(HEAD_DIM, HEAD_DIM)], w_sem.at[1])
    wq_copy = pltpu.make_async_copy(wq_hbm, wq, w_sem.at[2])
    wo_copy = pltpu.make_async_copy(wo_hbm, wo, w_sem.at[3])
    for copy in tok_copies + [wk_copy, wv_copy, wq_copy, wo_copy]:
        copy.start()

    barrier = pltpu.get_barrier_semaphore()
    for where in ({"seq": z_next}, {"seq": z_prev}, {"seq": right}, {"seq": left},
                  {"tp": x_right}, {"tp": x_left}, {"tp": sib}):
        pl.semaphore_signal(barrier, inc=1, device_id=where, device_id_type=pl.DeviceIdType.MESH)

    def norm_rows(i, carry):
        at = pl.ds(pl.multiple_of(i * 16, 16), 16)
        x = xs[at, :].astype(F32)
        scale = lax.rsqrt(jnp.mean(x * x, axis=-1, keepdims=True) + 1e-05)
        nrm[at, :] = (x * scale * gain_ref[...]).astype(BF16)
        return carry

    for i in range(TILES):
        tok_copies[i].wait()
        lax.fori_loop(i * (tile // 16), (i + 1) * (tile // 16), norm_rows, 0)

    def rotate(x, cosine, sine):
        return x * cosine + pltpu.roll(x, HEAD_DIM // 2, 1) * sine

    wk_copy.wait()
    wv_copy.wait()
    half = rows // 2
    for i in range(2):
        at = pl.ds(i * half, half)
        both = jnp.dot(nrm[at, :], wkv[...], preferred_element_type=F32)
        kv[0, at, :HEAD_DIM] = rotate(both[:, :HEAD_DIM], cos_ref[at, :], sin_ref[at, :]).astype(BF16)
        kv[0, at, HEAD_DIM:] = both[:, HEAD_DIM:].astype(BF16)

    pl.semaphore_wait(barrier, 7)

    def halo(message, source, where):
        return pltpu.make_async_remote_copy(
            src_ref=kv.at[source], dst_ref=kv.at[message],
            send_sem=ksend.at[message], recv_sem=krecv.at[message],
            device_id={"seq": where}, device_id_type=pl.DeviceIdType.MESH)

    halo(Z1, 0, z_next).start()

    @pl.when(y < 3)
    def _():
        halo(LA, 0, right).start()

    @pl.when(y == 0)
    def _():
        halo(RA, 0, left).start()

    wq_copy.wait()
    for pair in range(heads // 2):
        both = jnp.dot(nrm[...], wq[:, pair * 256:(pair + 1) * 256], preferred_element_type=F32)
        for j in range(2):
            h = pair * 2 + j
            q = rotate(both[:, j * 128:(j + 1) * 128], cos_ref[...], sin_ref[...]).astype(BF16)
            for t in range(TILES):
                qs[t, h * tile:(h + 1) * tile, :] = q[t * tile:(t + 1) * tile, :]

    factor = math.log2(math.e) / math.sqrt(HEAD_DIM)
    lanes = lax.broadcasted_iota(jnp.int32, (tile, HEAD_DIM), 1)
    ones = jnp.ones((rows, HEAD_DIM), BF16)
    column = lambda steps: lax.rem(y + steps + 4, 4)
    back = [0, 1, 2, pick(y, (2, 0, 0, 0)), 1, pick(y, (2, 2, 2, 0)), 1,
            pick(y, (1, 1, 0, 0)), pick(y, (2, 2, 1, 1))]
    side = [0, 0, 0, -1, -1, 1, 1, -2, 2]
    starts = [((z - back[s]) * 4 + column(side[s])) * rows for s in range(9)]

    def start_of(slot):
        value = starts[8]
        for s in range(7, -1, -1):
            value = jnp.where(slot == s, starts[s], value)
        return value

    def unit(t, slot, first):
        k = kv[slot, :, :HEAD_DIM]
        v = jnp.concatenate([kv[slot, :, HEAD_DIM:], ones], axis=1)
        low = lo_ref[pl.ds(pl.multiple_of(t * tile, tile), tile), :] - start_of(slot)
        s = lax.dot_general(qs[t], k, (((1,), (1,)), ((), ())), preferred_element_type=F32)
        keep = []
        for c in range(rows // 128):
            ok = lanes + c * 128 >= low
            if first:
                mine = lax.broadcasted_iota(jnp.int32, (tile, HEAD_DIM), 0) + t * tile
                ok = ok & (lanes + c * 128 <= mine)
            keep.append(ok)
        chunks = []
        for c in range(rows // 128):
            part = s[:, c * 128:(c + 1) * 128]
            part = jnp.concatenate(
                [jnp.where(keep[c], part[h * tile:(h + 1) * tile], F32(-1e30)) for h in range(heads)], axis=0)
            chunks.append(part)
        top = chunks[0]
        for part in chunks[1:]:
            top = jnp.maximum(top, part)
        peak = jnp.max(top, axis=1, keepdims=True) * factor
        peak = jnp.broadcast_to(peak, (heads * tile, HEAD_DIM))
        if not first:
            old = m_s[t]
            peak = jnp.maximum(old, peak)
        p = jnp.concatenate([jnp.exp2(part * factor - peak).astype(BF16) for part in chunks], axis=1)
        new = jnp.dot(p, v, preferred_element_type=F32)
        m_s[t] = peak
        if first:
            acc[t] = new
        else:
            decay = jnp.exp2(old - peak)
            acc[t, :, :HEAD_DIM] = acc[t, :, :HEAD_DIM] * decay + new[:, :HEAD_DIM]
            acc[t, :, HEAD_DIM:] = acc[t, :, HEAD_DIM:] * decay + new[:, HEAD_DIM:]

    def sweep(slot, first=False):
        def body(t, carry):
            unit(t, slot, first)
            return carry
        lax.fori_loop(0, TILES, body, 0)

    order = [pick(y, options) for options in zip(
        (Z1, Z2, L1, R1, LA, RA, LX, RX),
        (Z1, LA, Z2, L1, R1, RA, LX, RX),
        (Z1, LA, Z2, L1, R1, RA, LX, RX),
        (Z1, LA, RA, Z2, L1, R1, LX, RX))]
    inner = (y == 1) | (y == 2)
    relay_right = jnp.where(inner, LA, L1)
    relay_left = jnp.where(inner, RA, R1)

    def arrive(step):
        slot = order[step]
        halo(slot, slot, right).wait_recv()
        if step == 0:
            halo(Z2, Z1, z_next).start()
            halo(L1, Z1, right).start()
            halo(R1, Z1, left).start()
            return slot

        @pl.when((slot == Z2) & (y > 0))
        def _():
            halo(RA, Z2, left).start()

        @pl.when((slot == Z2) & (y == 3))
        def _():
            halo(LA, Z2, right).start()

        @pl.when(slot == relay_right)
        def _():
            halo(LX, relay_right, right).start()

        @pl.when(slot == relay_left)
        def _():
            halo(RX, relay_left, left).start()

        return slot

    sweep(0, True)
    for step in range(8 - NB):
        sweep(arrive(step))
    last = [arrive(step) for step in range(8 - NB, 8)]

    half_tile = tile // 2
    upper, lower = pl.ds(0, half_tile), pl.ds(half_tile, half_tile)
    everything = pl.ds(0, tile)
    gather_plan = (
        (0, 1, everything, x_right), (0, 2, everything, x_left), (0, 4, everything, sib),
        (1, 3, upper, x_right), (2, 3, lower, x_left),
        (1, 5, everything, sib), (2, 6, everything, sib),
        (3, 7, upper, sib), (3, 7, lower, sib))

    def gather(t, message):
        source, target, part, where = gather_plan[message]
        return pltpu.make_async_remote_copy(
            src_ref=gb.at[t, source, part], dst_ref=gb.at[t, target, part],
            send_sem=gsend.at[t, message], recv_sem=grecv.at[t, message],
            device_id={"tp": where}, device_id_type=pl.DeviceIdType.MESH)

    def finish(t):
        result = (acc[t, :, :HEAD_DIM] / acc[t, :, HEAD_DIM:]).astype(BF16)
        for h in range(heads):
            gb[t, 0, :, h * 128:(h + 1) * 128] = result[h * tile:(h + 1) * tile]
        for message in (0, 1, 2):
            gather(t, message).start()

    def relay(t):
        gather(t, 0).wait_recv()
        gather(t, 3).start()
        gather(t, 5).start()
        gather(t, 1).wait_recv()
        gather(t, 4).start()
        gather(t, 6).start()

    def across(t):
        gather(t, 3).wait_recv()
        gather(t, 7).start()
        gather(t, 4).wait_recv()
        gather(t, 8).start()

    flip = lambda index: index + 1 - 2 * core
    owners = (tp, x_left, x_right, opposite, sib, flip(x_left), flip(x_right), flip(opposite))
    part_width = heads * HEAD_DIM

    def project(t):
        for message in (2, 5, 6, 7, 8):
            gather(t, message).wait_recv()
        total = jnp.zeros((tile, out_ref.shape[1]), F32)
        for i in range(8):
            at = pl.ds(pl.multiple_of(owners[i] * part_width, part_width), part_width)
            total += jnp.dot(gb[t, i], wo[at, :], preferred_element_type=F32)
        out_ref[pl.ds(pl.multiple_of(t * tile, tile), tile), :] = total.astype(BF16)

    wo_copy.wait()
    for t in range(TILES):
        for slot in last:
            unit(t, slot, False)
        finish(t)
        if t >= 1:
            relay(t - 1)
        if t >= 2:
            across(t - 2)
    project(0)
    relay(3)
    across(2)
    project(1)
    across(3)
    project(2)
    project(3)

    for t in range(TILES):
        for message in range(9):
            gather(t, message).wait_send()
    for message in range(1, 9):
        halo(message, message, right).wait_send()


def shards(tokens, norm_gain, query_weight, key_weight, value_weight, out_weight, segments):
    rows, width = tokens.shape
    heads = query_weight.shape[1] // HEAD_DIM
    first = lax.axis_index("seq") * rows
    indices = first + jnp.arange(rows, dtype=jnp.int32)
    half = HEAD_DIM // 2
    freqs = 10000.0 ** (-(jnp.arange(half, dtype=F32) * 2.0 / HEAD_DIM))
    angles = indices.astype(F32)[:, None] * freqs[None, :]
    cosine, sine = jnp.cos(angles), jnp.sin(angles)
    cosine = jnp.concatenate([cosine, cosine], axis=1)
    sine = jnp.concatenate([-sine, sine], axis=1)
    mine = lax.dynamic_slice_in_dim(segments, first, rows, 0)
    one = jnp.sum((segments < 1).astype(jnp.int32))
    two = jnp.sum((segments < 2).astype(jnp.int32))
    begin = jnp.where(mine == 0, 0, jnp.where(mine == 1, one, two))
    low = jnp.maximum(indices - (WINDOW - 1), begin)
    low = jnp.broadcast_to(low[:, None], (rows, HEAD_DIM))
    tile = rows // TILES
    vmem = pl.BlockSpec(memory_space=pltpu.VMEM)
    hbm = pl.BlockSpec(memory_space=pl.ANY)
    return pl.pallas_call(
        kernel,
        out_shape=jax.ShapeDtypeStruct((rows, out_weight.shape[1]), BF16),
        in_specs=[hbm, vmem, vmem, vmem, vmem, hbm, hbm, hbm, hbm],
        out_specs=vmem,
        scratch_shapes=[
            pltpu.VMEM((rows, width), BF16),
            pltpu.VMEM((rows, width), BF16),
            pltpu.VMEM(query_weight.shape, BF16),
            pltpu.VMEM((width, 2 * HEAD_DIM), BF16),
            pltpu.VMEM(out_weight.shape, BF16),
            pltpu.VMEM((9, rows, 2 * HEAD_DIM), BF16),
            pltpu.VMEM((TILES, heads * tile, HEAD_DIM), BF16),
            pltpu.VMEM((TILES, heads * tile, HEAD_DIM), F32),
            pltpu.VMEM((TILES, heads * tile, 2 * HEAD_DIM), F32),
            pltpu.VMEM((TILES, 8, tile, heads * HEAD_DIM), BF16),
            pltpu.SemaphoreType.DMA((TILES,)),
            pltpu.SemaphoreType.DMA((4,)),
            pltpu.SemaphoreType.DMA((9,)),
            pltpu.SemaphoreType.DMA((9,)),
            pltpu.SemaphoreType.DMA((TILES, 9)),
            pltpu.SemaphoreType.DMA((TILES, 9)),
        ],
        compiler_params=pltpu.CompilerParams(
            collective_id=0, has_side_effects=True, vmem_limit_bytes=56 << 20),
    )(tokens, norm_gain[None, :], cosine, sine, low, query_weight, key_weight, value_weight, out_weight)


def solution(mesh):
    return jax.shard_map(
        shards,
        mesh=mesh,
        in_specs=(
            P("seq", None),
            P(),
            P(None, "tp"),
            P(None, "tp"),
            P(None, "tp"),
            P(None, "tp"),
            P(),
        ),
        out_specs=P("seq", "tp"),
        check_vma=False,
    )
```

```python
import math

import jax
import jax.numpy as jnp
from jax import lax
from jax.experimental import pallas as pl
from jax.experimental.pallas import tpu as pltpu
from jax.sharding import PartitionSpec as P

HEAD_DIM = 128
WINDOW = 4096
TILES = 4
NB = 2
Z1, Z2, LA, L1, RA, R1, LX, RX = range(1, 9)
F32 = jnp.float32
BF16 = jnp.bfloat16


def pick(y, options):
    value = jnp.int32(options[3])
    for i in (2, 1, 0):
        value = jnp.where(y == i, jnp.int32(options[i]), value)
    return value


def kernel(tok_hbm, gain_ref, freq_ref, seg_ref, wq_hbm, wk_hbm, wv_hbm, wo_hbm, out_ref,
           xs, nrm, wq, wkv, wo, kv, qs, m_s, acc, gb, cos_s, sin_s, low_s,
           tok_sem, w_sem, ksend, krecv, gsend, grecv):
    rows, width = xs.shape
    heads = wq.shape[1] // HEAD_DIM
    tile = rows // TILES
    half = rows // 2
    seq = lax.axis_index("seq")
    tp = lax.axis_index("tp")
    y = lax.rem(seq, 4)
    z = seq // 4
    z_last = lax.axis_size("seq") // 4 - 1
    row0 = z * 4
    z_next = lax.rem(seq + 4, 32)
    z_prev = lax.rem(seq + 28, 32)
    right = row0 + lax.rem(y + 1, 4)
    left = row0 + lax.rem(y + 3, 4)
    core = lax.rem(tp, 2)
    x_right = lax.rem(tp + 2, 8)
    x_left = lax.rem(tp + 6, 8)
    sib = tp + 1 - 2 * core
    opposite = lax.rem(tp + 4, 8)

    tok_copies = [
        pltpu.make_async_copy(tok_hbm.at[pl.ds(i * tile, tile)], xs.at[pl.ds(i * tile, tile)], tok_sem.at[i])
        for i in range(TILES)
    ]
    wk_copy = pltpu.make_async_copy(wk_hbm, wkv.at[:, pl.ds(0, HEAD_DIM)], w_sem.at[0])
    wv_copy = pltpu.make_async_copy(wv_hbm, wkv.at[:, pl.ds(HEAD_DIM, HEAD_DIM)], w_sem.at[1])
    wq_copy = pltpu.make_async_copy(wq_hbm, wq, w_sem.at[2])
    wo_copy = pltpu.make_async_copy(wo_hbm, wo, w_sem.at[3])
    for copy in tok_copies[:2] + [wk_copy, wv_copy] + tok_copies[2:] + [wq_copy, wo_copy]:
        copy.start()

    barrier = pltpu.get_barrier_semaphore()
    for where in ({"seq": z_next}, {"seq": z_prev}, {"seq": right}, {"seq": left},
                  {"tp": x_right}, {"tp": x_left}, {"tp": sib}):
        pl.semaphore_signal(barrier, inc=1, device_id=where, device_id_type=pl.DeviceIdType.MESH)

    def count_below(value):
        hits = (seg_ref[...] < value).astype(F32)
        return jnp.sum(jnp.sum(hits, axis=0, keepdims=True), axis=1, keepdims=True).astype(jnp.int32)

    second, third = count_below(1), count_below(2)

    def tables(i, carry):
        at = pl.ds(pl.multiple_of(i * 64, 64), 64)
        position = seq * rows + i * 64 + lax.broadcasted_iota(jnp.int32, (64, HEAD_DIM), 0)
        angle = position.astype(F32) * freq_ref[...]
        lane = lax.broadcasted_iota(jnp.int32, (64, HEAD_DIM), 1)
        sine = jnp.sin(angle)
        cos_s[at, :] = jnp.cos(angle)
        sin_s[at, :] = jnp.where(lane < HEAD_DIM // 2, -sine, sine)
        begin = jnp.where(position < second, 0, jnp.where(position < third, second, third))
        low_s[at, :] = jnp.maximum(position - (WINDOW - 1), begin)
        return carry

    lax.fori_loop(0, rows // 64, tables, 0)

    back = [0, 1, 2, pick(y, (2, 0, 0, 0)), 1, pick(y, (2, 2, 2, 0)), 1,
            pick(y, (1, 1, 0, 0)), pick(y, (2, 2, 1, 1))]
    side = [0, 0, 0, -1, -1, 1, 1, -2, 2]
    starts = [((z - back[s]) * 4 + lax.rem(y + side[s] + 4, 4)) * rows for s in range(9)]
    for s in range(1, 9):
        @pl.when(z < back[s])
        def _():
            kv[s] = jnp.zeros(kv.shape[1:], BF16)

    def norm_rows(i, carry):
        at = pl.ds(pl.multiple_of(i * 16, 16), 16)
        x = xs[at, :].astype(F32)
        scale = lax.rsqrt(jnp.mean(x * x, axis=-1, keepdims=True) + 1e-05)
        nrm[at, :] = (x * scale * gain_ref[...]).astype(BF16)
        return carry

    def rotate(x, cosine, sine):
        return x * cosine + pltpu.roll(x, HEAD_DIM // 2, 1) * sine

    def halo(message, source, where, c):
        part = pl.ds(c * half, half)
        return pltpu.make_async_remote_copy(
            src_ref=kv.at[source, part], dst_ref=kv.at[message, part],
            send_sem=ksend.at[message, c], recv_sem=krecv.at[message, c],
            device_id={"seq": where}, device_id_type=pl.DeviceIdType.MESH)

    def send(condition, message, source, where, c):
        @pl.when(condition)
        def _():
            halo(message, source, where, c).start()

    def got(message, c, condition=None):
        valid = z >= back[message]
        @pl.when(valid if condition is None else valid & condition)
        def _():
            halo(message, message, right, c).wait_recv()

    for c in range(2):
        for i in range(c * TILES // 2, (c + 1) * TILES // 2):
            tok_copies[i].wait()
            lax.fori_loop(i * (tile // 16), (i + 1) * (tile // 16), norm_rows, 0, unroll=2)
        if c == 0:
            wk_copy.wait()
            wv_copy.wait()
        at = pl.ds(c * half, half)
        both = jnp.dot(nrm[at, :], wkv[...], preferred_element_type=F32)
        kv[0, at, :HEAD_DIM] = rotate(both[:, :HEAD_DIM], cos_s[at, :], sin_s[at, :]).astype(BF16)
        kv[0, at, HEAD_DIM:] = both[:, HEAD_DIM:].astype(BF16)
        if c == 0:
            pl.semaphore_wait(barrier, 7)
        send(z < z_last, Z1, 0, z_next, c)
        send(y < 3, LA, 0, right, c)
        send(y == 0, RA, 0, left, c)

    wq_copy.wait()
    for pair in range(heads // 2):
        both = jnp.dot(nrm[...], wq[:, pair * 256:(pair + 1) * 256], preferred_element_type=F32)
        for j in range(2):
            h = pair * 2 + j
            q = rotate(both[:, j * 128:(j + 1) * 128], cos_s[...], sin_s[...]).astype(BF16)
            for t in range(TILES):
                qs[t, h * tile:(h + 1) * tile, :] = q[t * tile:(t + 1) * tile, :]

    factor = math.log2(math.e) / math.sqrt(HEAD_DIM)
    lanes = lax.broadcasted_iota(jnp.int32, (tile, HEAD_DIM), 1)
    ones = jnp.ones((rows, HEAD_DIM), BF16)

    def start_of(slot):
        if isinstance(slot, int):
            return starts[slot]
        value = starts[8]
        for s in range(7, 0, -1):
            value = jnp.where(slot == s, starts[s], value)
        return value

    def unit(t, slot, first):
        k = kv[slot, :, :HEAD_DIM]
        v = jnp.concatenate([kv[slot, :, HEAD_DIM:], ones], axis=1)
        low = low_s[t * tile:(t + 1) * tile, :] - start_of(slot)
        s = lax.dot_general(qs[t], k, (((1,), (1,)), ((), ())), preferred_element_type=F32)
        chunks = []
        for c in range(rows // 128):
            ok = lanes + c * 128 >= low
            if first:
                mine = lax.broadcasted_iota(jnp.int32, (tile, HEAD_DIM), 0) + t * tile
                ok = ok & (lanes + c * 128 <= mine)
            part = s[:, c * 128:(c + 1) * 128]
            chunks.append(jnp.concatenate(
                [jnp.where(ok, part[h * tile:(h + 1) * tile], F32(-1e30)) for h in range(heads)], axis=0))
        top = chunks[0]
        for part in chunks[1:]:
            top = jnp.maximum(top, part)
        peak = jnp.max(top, axis=1, keepdims=True) * factor
        peak = jnp.broadcast_to(peak, (heads * tile, HEAD_DIM))
        if not first:
            old = m_s[t]
            peak = jnp.maximum(old, peak)
        p = jnp.concatenate([jnp.exp2(part * factor - peak).astype(BF16) for part in chunks], axis=1)
        new = jnp.dot(p, v, preferred_element_type=F32)
        m_s[t] = peak
        if first:
            acc[t] = new
        else:
            decay = jnp.exp2(old - peak)
            acc[t, :, :HEAD_DIM] = acc[t, :, :HEAD_DIM] * decay + new[:, :HEAD_DIM]
            acc[t, :, HEAD_DIM:] = acc[t, :, HEAD_DIM:] * decay + new[:, HEAD_DIM:]

    def sweep(slot, first=False):
        for t in range(TILES):
            unit(t, slot, first)

    order = [pick(y, options) for options in zip(
        (Z1, R1, Z2, L1, RA, LA), (Z1, LA, R1, Z2, L1, RA),
        (Z1, LA, R1, Z2, L1, RA), (Z1, LA, RA, R1, Z2, L1))]
    inner = (y == 1) | (y == 2)
    outer = (y == 0) | (y == 3)

    def from_z1(c):
        got(Z1, c)
        send((z >= 1) & (z < z_last), Z2, Z1, z_next, c)
        send(z >= 1, L1, Z1, right, c)
        send(z >= 1, R1, Z1, left, c)

    def from_z2(c):
        got(Z2, c)
        send((z >= 2) & (y > 0), RA, Z2, left, c)
        send((z >= 2) & (y == 3), LA, Z2, right, c)

    def from_la(c):
        got(LA, c, inner)
        send(inner, LX, LA, right, c)

    def from_r1(c, condition):
        got(R1, c, condition)
        send(condition & outer & (z >= 1), RX, R1, left, c)

    def from_l1(c):
        got(L1, c)
        send(outer & (z >= 1), LX, L1, right, c)

    def from_ra(c, condition):
        got(RA, c, condition)
        send(condition & inner & (z >= 2), RX, RA, left, c)

    from_z1(0)
    sweep(0, True)
    from_z1(1)
    from_la(0)
    from_la(1)
    sweep(order[0])
    from_z2(0)
    from_r1(0, y >= 0)
    from_r1(1, y == 0)
    got(LA, 0, y == 3)
    got(LA, 1, y == 3)
    sweep(order[1])
    from_z2(1)
    from_r1(1, y > 0)
    from_l1(0)
    from_ra(0, y == 3)
    from_ra(1, y == 3)
    sweep(order[2])
    from_l1(1)
    sweep(order[3])
    from_ra(0, y < 3)
    from_ra(1, y == 0)
    sweep(order[4])
    from_ra(1, inner)
    got(LA, 0, y == 0)
    got(LA, 1, y == 0)
    sweep(order[5])
    last = (LX, RX)
    for slot in last:
        got(slot, 0)
        got(slot, 1)

    half_tile = tile // 2
    upper, lower = pl.ds(0, half_tile), pl.ds(half_tile, half_tile)
    everything = pl.ds(0, tile)
    gather_plan = (
        (0, 1, everything, x_right), (0, 2, everything, x_left), (0, 4, everything, sib),
        (1, 3, upper, x_right), (2, 3, lower, x_left),
        (1, 5, everything, sib), (2, 6, everything, sib),
        (3, 7, upper, sib), (3, 7, lower, sib))

    def gather(t, message):
        source, target, part, where = gather_plan[message]
        return pltpu.make_async_remote_copy(
            src_ref=gb.at[t, source, part], dst_ref=gb.at[t, target, part],
            send_sem=gsend.at[t, message], recv_sem=grecv.at[t, message],
            device_id={"tp": where}, device_id_type=pl.DeviceIdType.MESH)

    def finish(t):
        result = (acc[t, :, :HEAD_DIM] / acc[t, :, HEAD_DIM:]).astype(BF16)
        for h in range(heads):
            gb[t, 0, :, h * 128:(h + 1) * 128] = result[h * tile:(h + 1) * tile]
        for message in (0, 1, 2):
            gather(t, message).start()

    def relay(t):
        gather(t, 0).wait_recv()
        gather(t, 3).start()
        gather(t, 5).start()
        gather(t, 1).wait_recv()
        gather(t, 4).start()
        gather(t, 6).start()

    def across(t):
        gather(t, 3).wait_recv()
        gather(t, 7).start()
        gather(t, 4).wait_recv()
        gather(t, 8).start()

    flip = lambda index: index + 1 - 2 * core
    owners = (tp, x_left, x_right, opposite, sib, flip(x_left), flip(x_right), flip(opposite))
    part_width = heads * HEAD_DIM

    def partial(t, sources):
        total = None
        for i in sources:
            at = pl.ds(pl.multiple_of(owners[i] * part_width, part_width), part_width)
            term = jnp.dot(gb[t, i], wo[at, :], preferred_element_type=F32)
            total = term if total is None else total + term
        return total

    def project(t, early=None):
        for message in (7, 8):
            gather(t, message).wait_recv()
        total = partial(t, (3, 7)) + (partial_of(t) if early is None else early)
        out_ref[t * tile:(t + 1) * tile, :] = total.astype(BF16)

    def partial_of(t):
        for message in (2, 5, 6):
            gather(t, message).wait_recv()
        return partial(t, (0, 1, 2, 4, 5, 6))

    wo_copy.wait()
    for t in range(TILES):
        for slot in last:
            unit(t, slot, False)
        finish(t)
        if t >= 2:
            relay(t - 2)
    relay(2)
    across(0)
    project(0)
    relay(3)
    across(1)
    project(1)
    across(2)
    project(2)
    early = partial_of(3)
    across(3)
    project(3, early)

    for t in range(TILES):
        for message in range(9):
            gather(t, message).wait_send()
    sent = {Z1: z < z_last, Z2: (z >= 1) & (z < z_last), LA: (y < 3) | (z >= 2), L1: z >= 1,
            LX: inner | (z >= 1), RA: (y == 0) | (z >= 2), R1: z >= 1,
            RX: (outer & (z >= 1)) | (inner & (z >= 2))}
    for message, condition in sent.items():
        @pl.when(condition)
        def _():
            for c in range(2):
                halo(message, message, right, c).wait_send()


def shards(tokens, norm_gain, query_weight, key_weight, value_weight, out_weight, segments):
    rows, width = tokens.shape
    heads = query_weight.shape[1] // HEAD_DIM
    freqs = 10000.0 ** (-(jnp.arange(HEAD_DIM // 2, dtype=F32) * 2.0 / HEAD_DIM))
    freqs = jnp.concatenate([freqs, freqs])[None, :]
    tile = rows // TILES
    vmem = pl.BlockSpec(memory_space=pltpu.VMEM)
    hbm = pl.BlockSpec(memory_space=pl.ANY)
    return pl.pallas_call(
        kernel,
        out_shape=jax.ShapeDtypeStruct((rows, out_weight.shape[1]), BF16),
        in_specs=[hbm, vmem, vmem, vmem, hbm, hbm, hbm, hbm],
        out_specs=vmem,
        scratch_shapes=[
            pltpu.VMEM((rows, width), BF16),
            pltpu.VMEM((rows, width), BF16),
            pltpu.VMEM(query_weight.shape, BF16),
            pltpu.VMEM((width, 2 * HEAD_DIM), BF16),
            pltpu.VMEM(out_weight.shape, BF16),
            pltpu.VMEM((9, rows, 2 * HEAD_DIM), BF16),
            pltpu.VMEM((TILES, heads * tile, HEAD_DIM), BF16),
            pltpu.VMEM((TILES, heads * tile, HEAD_DIM), F32),
            pltpu.VMEM((TILES, heads * tile, 2 * HEAD_DIM), F32),
            pltpu.VMEM((TILES, 8, tile, heads * HEAD_DIM), BF16),
            pltpu.VMEM((rows, HEAD_DIM), F32),
            pltpu.VMEM((rows, HEAD_DIM), F32),
            pltpu.VMEM((rows, HEAD_DIM), jnp.int32),
            pltpu.SemaphoreType.DMA((TILES,)),
            pltpu.SemaphoreType.DMA((4,)),
            pltpu.SemaphoreType.DMA((9, 2)),
            pltpu.SemaphoreType.DMA((9, 2)),
            pltpu.SemaphoreType.DMA((TILES, 9)),
            pltpu.SemaphoreType.DMA((TILES, 9)),
        ],
        compiler_params=pltpu.CompilerParams(
            collective_id=0, has_side_effects=True, vmem_limit_bytes=56 << 20),
    )(tokens, norm_gain[None, :], freqs, segments.reshape(-1, HEAD_DIM),
      query_weight, key_weight, value_weight, out_weight)


def solution(mesh):
    return jax.shard_map(
        shards,
        mesh=mesh,
        in_specs=(
            P("seq", None),
            P(),
            P(None, "tp"),
            P(None, "tp"),
            P(None, "tp"),
            P(None, "tp"),
            P(),
        ),
        out_specs=P("seq", "tp"),
        check_vma=False,
    )
```

```python
import math

import jax
import jax.numpy as jnp
from jax import lax
from jax.experimental import pallas as pl
from jax.experimental.pallas import tpu as pltpu
from jax.sharding import PartitionSpec as P

HEAD_DIM = 128
WINDOW = 4096
TILES = 4
Z1, Z2, LA, L1, RA, R1, LX, RX = range(1, 9)
F32 = jnp.float32
BF16 = jnp.bfloat16


def pick(y, options):
    value = jnp.int32(options[3])
    for i in (2, 1, 0):
        value = jnp.where(y == i, jnp.int32(options[i]), value)
    return value


def kernel(tok_hbm, gain_ref, freq_ref, seg_ref, wq_hbm, wk_hbm, wv_hbm, wo_hbm, out_ref,
           xs, nrm, wq, wkv, wo, kv, qs, m_s, acc, gb, part, cos_s, sin_s, low_s,
           tok_sem, w_sem, ksend, krecv, gsend, grecv):
    rows, width = xs.shape
    heads = wq.shape[1] // HEAD_DIM
    tile = rows // TILES
    seq = lax.axis_index("seq")
    tp = lax.axis_index("tp")
    y = lax.rem(seq, 4)
    z = seq // 4
    z_last = lax.axis_size("seq") // 4 - 1
    row0 = z * 4
    z_next = lax.rem(seq + 4, 32)
    z_prev = lax.rem(seq + 28, 32)
    right = row0 + lax.rem(y + 1, 4)
    left = row0 + lax.rem(y + 3, 4)
    core = lax.rem(tp, 2)
    x_right = lax.rem(tp + 2, 8)
    x_left = lax.rem(tp + 6, 8)
    sib = tp + 1 - 2 * core
    opposite = lax.rem(tp + 4, 8)

    tok_copies = [
        pltpu.make_async_copy(tok_hbm.at[pl.ds(i * tile, tile)], xs.at[pl.ds(i * tile, tile)], tok_sem.at[i])
        for i in range(TILES)
    ]
    wk_copy = pltpu.make_async_copy(wk_hbm, wkv.at[:, pl.ds(0, HEAD_DIM)], w_sem.at[0])
    wv_copy = pltpu.make_async_copy(wv_hbm, wkv.at[:, pl.ds(HEAD_DIM, HEAD_DIM)], w_sem.at[1])
    wq_copy = pltpu.make_async_copy(wq_hbm, wq, w_sem.at[2])
    wo_copy = pltpu.make_async_copy(wo_hbm, wo, w_sem.at[3])
    for copy in tok_copies[:2] + [wk_copy, wv_copy] + tok_copies[2:] + [wq_copy, wo_copy]:
        copy.start()

    barrier = pltpu.get_barrier_semaphore()
    for where in ({"seq": z_next}, {"seq": z_prev}, {"seq": right}, {"seq": left},
                  {"tp": x_right}, {"tp": x_left}, {"tp": sib}):
        pl.semaphore_signal(barrier, inc=1, device_id=where, device_id_type=pl.DeviceIdType.MESH)

    def count_below(value):
        hits = (seg_ref[...] < value).astype(F32)
        return jnp.sum(jnp.sum(hits, axis=0, keepdims=True), axis=1, keepdims=True).astype(jnp.int32)

    second, third = count_below(1), count_below(2)

    def tables(c):
        small = tile // 2
        shape = (small, HEAD_DIM)
        lane = lax.broadcasted_iota(jnp.int32, shape, 1)
        row = lax.broadcasted_iota(jnp.int32, shape, 0) + (seq * rows + c * tile)
        front = lane < HEAD_DIM // 2
        angle = jnp.where(front, row, row + small).astype(F32) * freq_ref[...]
        cosine, sine = jnp.cos(angle), jnp.sin(angle)
        other_cosine, other_sine = (pltpu.roll(value, HEAD_DIM // 2, 1) for value in (cosine, sine))
        for i in range(2):
            at = pl.ds(c * tile + i * small, small)
            mine = front if i == 0 else ~front
            turned = jnp.where(mine, sine, other_sine)
            cos_s[at, :] = jnp.where(mine, cosine, other_cosine)
            sin_s[at, :] = jnp.where(front, -turned, turned)
            position = row + i * small
            begin = jnp.where(position < second, 0, jnp.where(position < third, second, third))
            low_s[at, :] = jnp.maximum(position - (WINDOW - 1), begin)

    back = [0, 1, 2, pick(y, (2, 0, 0, 0)), 1, pick(y, (2, 2, 2, 0)), 1,
            pick(y, (1, 1, 0, 0)), pick(y, (2, 2, 1, 1))]
    side = [0, 0, 0, -1, -1, 1, 1, -2, 2]
    starts = [((z - back[s]) * 4 + lax.rem(y + side[s] + 4, 4)) * rows for s in range(9)]
    for s in range(1, 9):
        @pl.when(z < back[s])
        def _():
            kv[s] = jnp.zeros(kv.shape[1:], BF16)

    def norm_rows(i, carry):
        at = pl.ds(pl.multiple_of(i * 16, 16), 16)
        x = xs[at, :].astype(F32)
        scale = lax.rsqrt(jnp.mean(x * x, axis=-1, keepdims=True) + 1e-05)
        nrm[at, :] = (x * scale * gain_ref[...]).astype(BF16)
        return carry

    def rotate(x, cosine, sine):
        return x * cosine + pltpu.roll(x, HEAD_DIM // 2, 1) * sine

    sent = []

    def halo(message, source, where, c, used=None):
        part = pl.ds(c * tile, tile)
        return pltpu.make_async_remote_copy(
            src_ref=kv.at[source, part], dst_ref=kv.at[message, part],
            send_sem=ksend.at[message if used is None else used, c], recv_sem=krecv.at[message, c],
            device_id={"seq": where}, device_id_type=pl.DeviceIdType.MESH)

    def send(condition, message, source, where, c, used=None):
        sent.append((condition, message, c, used))

        @pl.when(condition)
        def _():
            halo(message, source, where, c, used).start()

    def got(message, c, condition=None):
        valid = z >= back[message]

        @pl.when(valid if condition is None else valid & condition)
        def _():
            halo(message, message, right, c).wait_recv()

    inner = (y == 1) | (y == 2)
    outer = (y == 0) | (y == 3)
    below = (z >= 1) & (z < z_last)

    def from_z1(c):
        got(Z1, c)
        send(below, Z2, Z1, z_next, c)
        send(z >= 1, R1, Z1, left, c)
        send(z >= 1, L1, Z1, right, c)

    def from_z2(c):
        got(Z2, c)
        send((z >= 2) & (y == 3), LA, Z2, right, c)

    def from_la(c):
        got(LA, c, inner)
        send(inner, LX, LA, right, c)

    def from_r1(c, condition):
        got(R1, c, condition)
        send(condition & (y < 3) & below, RA, R1, z_next, c, 9)
        if c >= TILES // 2:
            send(condition & (y == 1) & (z >= 1), LX, R1, left, c, 10)
        send(condition & outer & (z >= 1), RX, R1, left, c)

    def from_l1(c, condition):
        got(L1, c, condition)
        relays = outer if c < TILES // 2 else y == 0
        send(condition & relays & (z >= 1), LX, L1, right, c)

    def from_ra(c):
        got(RA, c, y < 3)
        send(inner & (z >= 2), RX, RA, left, c)

    tables(0)
    for c in range(TILES):
        tok_copies[c].wait()
        lax.fori_loop(c * (tile // 16), (c + 1) * (tile // 16), norm_rows, 0, unroll=2)
        if c == 0:
            wk_copy.wait()
            wv_copy.wait()
        else:
            tables(c)
        at = pl.ds(c * tile, tile)
        both = jnp.dot(nrm[at, :], wkv[...], preferred_element_type=F32)
        kv[0, at, :HEAD_DIM] = rotate(both[:, :HEAD_DIM], cos_s[at, :], sin_s[at, :]).astype(BF16)
        kv[0, at, HEAD_DIM:] = both[:, HEAD_DIM:].astype(BF16)
        if c == 0:
            pl.semaphore_wait(barrier, 7)
        send(z < z_last, Z1, 0, z_next, c)
        send(y < 3, LA, 0, right, c)
        send(y == 0, RA, 0, left, c)

    wq_copy.wait()
    for pair in range(heads // 2):
        both = jnp.dot(nrm[...], wq[:, pair * 256:(pair + 1) * 256], preferred_element_type=F32)
        for j in range(2):
            h = pair * 2 + j
            q = rotate(both[:, j * 128:(j + 1) * 128], cos_s[...], sin_s[...]).astype(BF16)
            for t in range(TILES):
                qs[t, h * tile:(h + 1) * tile, :] = q[t * tile:(t + 1) * tile, :]
        from_z1(pair)

    factor = math.log2(math.e) / math.sqrt(HEAD_DIM)
    lanes = lax.broadcasted_iota(jnp.int32, (tile, HEAD_DIM), 1)
    ones = jnp.ones((rows, HEAD_DIM), BF16)

    def start_of(slot):
        if isinstance(slot, int):
            return starts[slot]
        value = starts[8]
        for s in range(7, 0, -1):
            value = jnp.where(slot == s, starts[s], value)
        return value

    def unit(t, slot, first):
        k = kv[slot, :, :HEAD_DIM]
        v = jnp.concatenate([kv[slot, :, HEAD_DIM:], ones], axis=1)
        low = low_s[t * tile:(t + 1) * tile, :] - start_of(slot)
        s = lax.dot_general(qs[t], k, (((1,), (1,)), ((), ())), preferred_element_type=F32)
        chunks = []
        for c in range(rows // 128):
            ok = lanes + c * 128 >= low
            if first:
                mine = lax.broadcasted_iota(jnp.int32, (tile, HEAD_DIM), 0) + t * tile
                ok = ok & (lanes + c * 128 <= mine)
            part = s[:, c * 128:(c + 1) * 128]
            chunks.append(jnp.concatenate(
                [jnp.where(ok, part[h * tile:(h + 1) * tile], F32(-1e30)) for h in range(heads)], axis=0))
        top = chunks[0]
        for part in chunks[1:]:
            top = jnp.maximum(top, part)
        peak = jnp.max(top, axis=1, keepdims=True) * factor
        peak = jnp.broadcast_to(peak, (heads * tile, HEAD_DIM))
        if not first:
            old = m_s[t]
            peak = jnp.maximum(old, peak)
        p = jnp.concatenate([jnp.exp2(part * factor - peak).astype(BF16) for part in chunks], axis=1)
        new = jnp.dot(p, v, preferred_element_type=F32)
        m_s[t] = peak
        if first:
            acc[t] = new
        else:
            decay = jnp.exp2(old - peak)
            acc[t, :, :HEAD_DIM] = acc[t, :, :HEAD_DIM] * decay + new[:, :HEAD_DIM]
            acc[t, :, HEAD_DIM:] = acc[t, :, HEAD_DIM:] * decay + new[:, HEAD_DIM:]

    def sweep(slot, first=False):
        for t in range(TILES):
            unit(t, slot, first)

    order = [pick(y, options) for options in zip(
        (Z1, R1, L1, Z2, LA, RA), (Z1, LA, R1, Z2, L1, RA),
        (Z1, LA, R1, Z2, L1, RA), (Z1, LA, RA, R1, Z2, L1))]
    always = y >= 0

    def got_all(message, condition=None):
        for c in range(TILES):
            got(message, c, condition)

    sweep(0, True)
    from_z1(2)
    from_z1(3)
    for c in range(TILES):
        from_la(c)
    sweep(order[0])
    from_r1(0, always)
    from_r1(1, always)
    from_z2(0)
    from_r1(2, y == 0)
    from_r1(3, y == 0)
    got_all(LA, y == 3)
    sweep(order[1])
    from_r1(2, y > 0)
    from_z2(1)
    from_l1(0, always)
    from_l1(1, always)
    from_r1(3, y > 0)
    from_l1(2, y == 0)
    from_l1(3, y == 0)
    got_all(RA, y == 3)
    sweep(order[2])
    from_z2(2)
    from_l1(2, y > 0)
    from_z2(3)
    from_l1(3, y > 0)
    sweep(order[3])
    from_ra(0)
    got_all(LA, y == 0)
    sweep(order[4])
    from_ra(1)
    from_ra(2)
    from_ra(3)
    sweep(order[5])
    got_all(LX)
    sweep(LX)
    got_all(RX)

    half_tile = tile // 2
    upper, lower = pl.ds(0, half_tile), pl.ds(half_tile, half_tile)
    everything = pl.ds(0, tile)
    gather_plan = (
        (0, 1, everything, x_right), (0, 2, everything, x_left), (0, 4, everything, sib),
        (1, 3, upper, x_right), (2, 3, lower, x_left),
        (1, 5, everything, sib), (2, 6, everything, sib),
        (3, 7, upper, sib), (3, 7, lower, sib))

    def gather(t, message):
        source, target, part, where = gather_plan[message]
        return pltpu.make_async_remote_copy(
            src_ref=gb.at[t, source, part], dst_ref=gb.at[t, target, part],
            send_sem=gsend.at[t, message], recv_sem=grecv.at[t, message],
            device_id={"tp": where}, device_id_type=pl.DeviceIdType.MESH)

    def finish(t):
        result = (acc[t, :, :HEAD_DIM] / acc[t, :, HEAD_DIM:]).astype(BF16)
        for h in range(heads):
            gb[t, 0, :, h * 128:(h + 1) * 128] = result[h * tile:(h + 1) * tile]
        for message in (0, 1, 2):
            gather(t, message).start()

    def relay(t):
        gather(t, 0).wait_recv()
        gather(t, 3).start()
        gather(t, 5).start()
        gather(t, 1).wait_recv()
        gather(t, 4).start()
        gather(t, 6).start()

    def across(t):
        gather(t, 3).wait_recv()
        gather(t, 7).start()
        gather(t, 4).wait_recv()
        gather(t, 8).start()

    flip = lambda index: index + 1 - 2 * core
    owners = (tp, x_left, x_right, opposite, sib, flip(x_left), flip(x_right), flip(opposite))
    part_width = heads * HEAD_DIM

    def partial(t, sources):
        total = None
        for i in sources:
            at = pl.ds(pl.multiple_of(owners[i] * part_width, part_width), part_width)
            term = jnp.dot(gb[t, i], wo[at, :], preferred_element_type=F32)
            total = term if total is None else total + term
        return total

    def begin(t):
        for message in (2, 5, 6):
            gather(t, message).wait_recv()
        part[t] = partial(t, (0, 1, 2, 4, 5, 6))

    def project(t):
        for message in (7, 8):
            gather(t, message).wait_recv()
        out_ref[t * tile:(t + 1) * tile, :] = (part[t] + partial(t, (3, 7))).astype(BF16)

    wo_copy.wait()
    for t in range(TILES):
        unit(t, RX, False)
        finish(t)
    relay(0)
    relay(1)
    begin(0)
    relay(2)
    begin(1)
    relay(3)
    begin(2)
    across(0)
    begin(3)
    across(1)
    project(0)
    across(2)
    project(1)
    across(3)
    project(2)
    project(3)

    for t in range(TILES):
        for message in range(9):
            gather(t, message).wait_send()
    for condition, message, c, used in sent:
        @pl.when(condition)
        def _():
            halo(message, message, right, c, used).wait_send()


def shards(tokens, norm_gain, query_weight, key_weight, value_weight, out_weight, segments):
    rows, width = tokens.shape
    heads = query_weight.shape[1] // HEAD_DIM
    freqs = 10000.0 ** (-(jnp.arange(HEAD_DIM // 2, dtype=F32) * 2.0 / HEAD_DIM))
    freqs = jnp.concatenate([freqs, freqs])[None, :]
    tile = rows // TILES
    vmem = pl.BlockSpec(memory_space=pltpu.VMEM)
    hbm = pl.BlockSpec(memory_space=pl.ANY)
    return pl.pallas_call(
        kernel,
        out_shape=pltpu.VMEM((rows, out_weight.shape[1]), BF16),
        in_specs=[hbm, vmem, vmem, vmem, hbm, hbm, hbm, hbm],
        out_specs=vmem,
        scratch_shapes=[
            pltpu.VMEM((rows, width), BF16),
            pltpu.VMEM((rows, width), BF16),
            pltpu.VMEM(query_weight.shape, BF16),
            pltpu.VMEM((width, 2 * HEAD_DIM), BF16),
            pltpu.VMEM(out_weight.shape, BF16),
            pltpu.VMEM((9, rows, 2 * HEAD_DIM), BF16),
            pltpu.VMEM((TILES, heads * tile, HEAD_DIM), BF16),
            pltpu.VMEM((TILES, heads * tile, HEAD_DIM), F32),
            pltpu.VMEM((TILES, heads * tile, 2 * HEAD_DIM), F32),
            pltpu.VMEM((TILES, 8, tile, heads * HEAD_DIM), BF16),
            pltpu.VMEM((TILES, tile, out_weight.shape[1]), F32),
            pltpu.VMEM((rows, HEAD_DIM), F32),
            pltpu.VMEM((rows, HEAD_DIM), F32),
            pltpu.VMEM((rows, HEAD_DIM), jnp.int32),
            pltpu.SemaphoreType.DMA((TILES,)),
            pltpu.SemaphoreType.DMA((4,)),
            pltpu.SemaphoreType.DMA((11, TILES)),
            pltpu.SemaphoreType.DMA((9, TILES)),
            pltpu.SemaphoreType.DMA((TILES, 9)),
            pltpu.SemaphoreType.DMA((TILES, 9)),
        ],
        compiler_params=pltpu.CompilerParams(
            collective_id=0, has_side_effects=True, vmem_limit_bytes=56 << 20),
    )(tokens, norm_gain[None, :], freqs, segments.reshape(-1, HEAD_DIM),
      query_weight, key_weight, value_weight, out_weight)


def solution(mesh):
    return jax.shard_map(
        shards,
        mesh=mesh,
        in_specs=(
            P("seq", None),
            P(),
            P(None, "tp"),
            P(None, "tp"),
            P(None, "tp"),
            P(None, "tp"),
            P(),
        ),
        out_specs=P("seq", "tp"),
        check_vma=False,
    )
```

```python
import math

import jax
import jax.numpy as jnp
from jax import lax
from jax.experimental import pallas as pl
from jax.experimental.pallas import tpu as pltpu
from jax.sharding import PartitionSpec as P

HEAD_DIM = 128
WINDOW = 4096
TILES = 4
Z1, Z2, LA, L1, RA, R1, LX, RX = range(1, 9)
F32 = jnp.float32
BF16 = jnp.bfloat16


def pick(y, options):
    value = jnp.int32(options[3])
    for i in (2, 1, 0):
        value = jnp.where(y == i, jnp.int32(options[i]), value)
    return value


def kernel(tok_hbm, gain_ref, freq_ref, seg_ref, wq_hbm, wk_hbm, wv_hbm, wo_hbm, out_ref,
           xs, nrm, wq, wkv, wo, kv, qs, m_s, acc, gb, part, cos_s, sin_s, low_s,
           tok_sem, w_sem, ksend, krecv, gsend, grecv):
    rows, width = xs.shape
    heads = wq.shape[1] // HEAD_DIM
    tile = rows // TILES
    seq = lax.axis_index("seq")
    tp = lax.axis_index("tp")
    y = lax.rem(seq, 4)
    z = seq // 4
    z_last = lax.axis_size("seq") // 4 - 1
    row0 = z * 4
    z_next = lax.rem(seq + 4, 32)
    z_prev = lax.rem(seq + 28, 32)
    right = row0 + lax.rem(y + 1, 4)
    left = row0 + lax.rem(y + 3, 4)
    core = lax.rem(tp, 2)
    x_right = lax.rem(tp + 2, 8)
    x_left = lax.rem(tp + 6, 8)
    sib = tp + 1 - 2 * core
    opposite = lax.rem(tp + 4, 8)

    tok_copies = [
        pltpu.make_async_copy(tok_hbm.at[pl.ds(i * tile, tile)], xs.at[pl.ds(i * tile, tile)], tok_sem.at[i])
        for i in range(TILES)
    ]
    wk_copy = pltpu.make_async_copy(wk_hbm, wkv.at[:, pl.ds(0, HEAD_DIM)], w_sem.at[0])
    wv_copy = pltpu.make_async_copy(wv_hbm, wkv.at[:, pl.ds(HEAD_DIM, HEAD_DIM)], w_sem.at[1])
    wq_copy = pltpu.make_async_copy(wq_hbm, wq, w_sem.at[2])
    wo_copy = pltpu.make_async_copy(wo_hbm, wo, w_sem.at[3])
    for copy in tok_copies[:2] + [wk_copy, wv_copy] + tok_copies[2:] + [wq_copy, wo_copy]:
        copy.start()

    barrier = pltpu.get_barrier_semaphore()
    for where in ({"seq": z_next}, {"seq": z_prev}, {"seq": right}, {"seq": left},
                  {"tp": x_right}, {"tp": x_left}, {"tp": sib}):
        pl.semaphore_signal(barrier, inc=1, device_id=where, device_id_type=pl.DeviceIdType.MESH)

    def count_below(value):
        hits = (seg_ref[...] < value).astype(F32)
        return jnp.sum(jnp.sum(hits, axis=0, keepdims=True), axis=1, keepdims=True).astype(jnp.int32)

    second, third = count_below(1), count_below(2)

    def tables(c):
        small = tile // 2
        shape = (small, HEAD_DIM)
        lane = lax.broadcasted_iota(jnp.int32, shape, 1)
        row = lax.broadcasted_iota(jnp.int32, shape, 0) + (seq * rows + c * tile)
        front = lane < HEAD_DIM // 2
        angle = jnp.where(front, row, row + small).astype(F32) * freq_ref[...]
        cosine, sine = jnp.cos(angle), jnp.sin(angle)
        other_cosine, other_sine = (pltpu.roll(value, HEAD_DIM // 2, 1) for value in (cosine, sine))
        for i in range(2):
            at = pl.ds(c * tile + i * small, small)
            mine = front if i == 0 else ~front
            turned = jnp.where(mine, sine, other_sine)
            cos_s[at, :] = jnp.where(mine, cosine, other_cosine)
            sin_s[at, :] = jnp.where(front, -turned, turned)
            position = row + i * small
            begin = jnp.where(position < second, 0, jnp.where(position < third, second, third))
            low_s[at, :] = jnp.maximum(position - (WINDOW - 1), begin)

    back = [0, 1, 2, pick(y, (2, 0, 0, 0)), 1, pick(y, (2, 2, 2, 0)), 1,
            pick(y, (1, 1, 0, 0)), pick(y, (2, 2, 1, 1))]
    side = [0, 0, 0, -1, -1, 1, 1, -2, 2]
    starts = [((z - back[s]) * 4 + lax.rem(y + side[s] + 4, 4)) * rows for s in range(9)]
    for s in range(1, 9):
        @pl.when(z < back[s])
        def _():
            kv[s] = jnp.zeros(kv.shape[1:], BF16)

    def norm_rows(i, carry):
        at = pl.ds(pl.multiple_of(i * 16, 16), 16)
        x = xs[at, :].astype(F32)
        scale = lax.rsqrt(jnp.mean(x * x, axis=-1, keepdims=True) + 1e-05)
        nrm[at, :] = (x * scale * gain_ref[...]).astype(BF16)
        return carry

    def rotate(x, cosine, sine):
        return x * cosine + pltpu.roll(x, HEAD_DIM // 2, 1) * sine

    sent = []

    def halo(message, source, where, c, used=None):
        part = pl.ds(c * tile, tile)
        return pltpu.make_async_remote_copy(
            src_ref=kv.at[source, part], dst_ref=kv.at[message, part],
            send_sem=ksend.at[message if used is None else used, c], recv_sem=krecv.at[message, c],
            device_id={"seq": where}, device_id_type=pl.DeviceIdType.MESH)

    def send(condition, message, source, where, c, used=None):
        sent.append((condition, message, c, used))

        @pl.when(condition)
        def _():
            halo(message, source, where, c, used).start()

    def got(message, c, condition=None):
        valid = z >= back[message]

        @pl.when(valid if condition is None else valid & condition)
        def _():
            halo(message, message, right, c).wait_recv()

    inner = (y == 1) | (y == 2)
    outer = (y == 0) | (y == 3)
    below = (z >= 1) & (z < z_last)

    def from_z1(c):
        got(Z1, c)
        send(below, Z2, Z1, z_next, c)
        send(z >= 1, R1, Z1, left, c)
        send(z >= 1, L1, Z1, right, c)

    def from_z2(c):
        got(Z2, c)
        if c < TILES // 2:
            send((z >= 2) & (y >= 2), RA, Z2, left, c)
        send((z >= 2) & (y == 3), LA, Z2, right, c)

    def from_la(c):
        got(LA, c, inner)
        send(inner, LX, LA, right, c)

    def from_r1(c, condition):
        got(R1, c, condition)
        send(condition & ((y == 0) if c < TILES // 2 else (y < 3)) & below, RA, R1, z_next, c, 9)
        if c >= TILES // 2:
            send(condition & (y == 1) & (z >= 1), LX, R1, left, c, 10)
        send(condition & outer & (z >= 1), RX, R1, left, c)

    def from_l1(c, condition):
        got(L1, c, condition)
        relays = outer if c < TILES // 2 else y == 0
        send(condition & relays & (z >= 1), LX, L1, right, c)

    def from_ra(c, condition):
        got(RA, c, condition)
        send(condition & (z >= 2), RX, RA, left, c)

    tables(0)
    for chunks in ((0,), (1,), (2, 3)):
        for c in chunks:
            tok_copies[c].wait()
            lax.fori_loop(c * (tile // 16), (c + 1) * (tile // 16), norm_rows, 0, unroll=2)
            if c == 0:
                wk_copy.wait()
                wv_copy.wait()
            else:
                tables(c)
        at = pl.ds(chunks[0] * tile, len(chunks) * tile)
        both = jnp.dot(nrm[at, :], wkv[...], preferred_element_type=F32)
        kv[0, at, :HEAD_DIM] = rotate(both[:, :HEAD_DIM], cos_s[at, :], sin_s[at, :]).astype(BF16)
        kv[0, at, HEAD_DIM:] = both[:, HEAD_DIM:].astype(BF16)
        if chunks[0] == 0:
            pl.semaphore_wait(barrier, 7)
        for c in chunks:
            send(z < z_last, Z1, 0, z_next, c)
            send(y < 3, LA, 0, right, c)
            send(y == 0, RA, 0, left, c)

    wq_copy.wait()
    for pair in range(heads // 2):
        both = jnp.dot(nrm[...], wq[:, pair * 256:(pair + 1) * 256], preferred_element_type=F32)
        for j in range(2):
            h = pair * 2 + j
            q = rotate(both[:, j * 128:(j + 1) * 128], cos_s[...], sin_s[...]).astype(BF16)
            for t in range(TILES):
                qs[t, h * tile:(h + 1) * tile, :] = q[t * tile:(t + 1) * tile, :]
    from_z1(0)

    factor = math.log2(math.e) / math.sqrt(HEAD_DIM)
    lanes = lax.broadcasted_iota(jnp.int32, (tile, HEAD_DIM), 1)
    ones = jnp.ones((rows, HEAD_DIM), BF16)

    def start_of(slot):
        if isinstance(slot, int):
            return starts[slot]
        value = starts[8]
        for s in range(7, 0, -1):
            value = jnp.where(slot == s, starts[s], value)
        return value

    def unit(t, slot, first):
        k = kv[slot, :, :HEAD_DIM]
        v = jnp.concatenate([kv[slot, :, HEAD_DIM:], ones], axis=1)
        low = low_s[t * tile:(t + 1) * tile, :] - start_of(slot)
        s = lax.dot_general(qs[t], k, (((1,), (1,)), ((), ())), preferred_element_type=F32)
        chunks = []
        for c in range(rows // 128):
            ok = lanes + c * 128 >= low
            if first:
                mine = lax.broadcasted_iota(jnp.int32, (tile, HEAD_DIM), 0) + t * tile
                ok = ok & (lanes + c * 128 <= mine)
            part = s[:, c * 128:(c + 1) * 128]
            chunks.append(jnp.concatenate(
                [jnp.where(ok, part[h * tile:(h + 1) * tile], F32(-1e30)) for h in range(heads)], axis=0))
        top = chunks[0]
        for part in chunks[1:]:
            top = jnp.maximum(top, part)
        peak = jnp.max(top, axis=1, keepdims=True) * factor
        peak = jnp.broadcast_to(peak, (heads * tile, HEAD_DIM))
        if not first:
            old = m_s[t]
            peak = jnp.maximum(old, peak)
        p = jnp.concatenate([jnp.exp2(part * factor - peak).astype(BF16) for part in chunks], axis=1)
        new = jnp.dot(p, v, preferred_element_type=F32)
        m_s[t] = peak
        if first:
            acc[t] = new
        else:
            decay = jnp.exp2(old - peak)
            acc[t, :, :HEAD_DIM] = acc[t, :, :HEAD_DIM] * decay + new[:, :HEAD_DIM]
            acc[t, :, HEAD_DIM:] = acc[t, :, HEAD_DIM:] * decay + new[:, HEAD_DIM:]

    def sweep(slot, first=False):
        for t in range(TILES):
            unit(t, slot, first)

    order = [pick(y, options) for options in zip(
        (Z1, R1, L1, Z2, LX, RA, LA), (Z1, LA, R1, Z2, L1, RA, LX),
        (Z1, LA, R1, Z2, L1, RA, LX), (Z1, LA, RA, R1, Z2, L1, LX))]
    always = y >= 0

    def got_all(message, condition=None):
        for c in range(TILES):
            got(message, c, condition)

    sweep(0, True)
    from_z1(1)
    from_z1(2)
    from_z1(3)
    for c in range(TILES):
        from_la(c)
    sweep(order[0])
    from_r1(0, always)
    from_r1(1, always)
    from_z2(0)
    from_r1(2, y == 0)
    from_r1(3, y == 0)
    got_all(LA, y == 3)
    sweep(order[1])
    from_z2(1)
    from_r1(2, y > 0)
    from_l1(0, always)
    from_l1(1, always)
    from_r1(3, y > 0)
    from_l1(2, y == 0)
    from_l1(3, y == 0)
    got_all(RA, y == 3)
    sweep(order[2])
    from_z2(2)
    from_l1(2, y > 0)
    from_z2(3)
    from_l1(3, y > 0)
    from_ra(0, inner)
    sweep(order[3])
    from_ra(1, inner)
    from_ra(2, inner)
    got_all(LX, y == 0)
    sweep(order[4])
    from_ra(3, inner)
    got_all(RA, y == 0)
    sweep(order[5])
    got_all(LX, y > 0)
    got_all(LA, y == 0)
    sweep(order[6])
    got_all(RX)

    half_tile = tile // 2
    upper, lower = pl.ds(0, half_tile), pl.ds(half_tile, half_tile)
    everything = pl.ds(0, tile)
    gather_plan = (
        (0, 1, everything, x_right), (0, 2, everything, x_left), (0, 4, everything, sib),
        (1, 3, upper, x_right), (2, 3, lower, x_left),
        (1, 5, everything, sib), (2, 6, everything, sib),
        (3, 7, upper, sib), (3, 7, lower, sib))

    def gather(t, message):
        source, target, part, where = gather_plan[message]
        return pltpu.make_async_remote_copy(
            src_ref=gb.at[t, source, part], dst_ref=gb.at[t, target, part],
            send_sem=gsend.at[t, message], recv_sem=grecv.at[t, message],
            device_id={"tp": where}, device_id_type=pl.DeviceIdType.MESH)

    def finish(t):
        result = (acc[t, :, :HEAD_DIM] / acc[t, :, HEAD_DIM:]).astype(BF16)
        for h in range(heads):
            gb[t, 0, :, h * 128:(h + 1) * 128] = result[h * tile:(h + 1) * tile]
        for message in (0, 1, 2):
            gather(t, message).start()

    def relay(t):
        gather(t, 0).wait_recv()
        gather(t, 3).start()
        gather(t, 5).start()
        gather(t, 1).wait_recv()
        gather(t, 4).start()
        gather(t, 6).start()

    def across(t):
        gather(t, 3).wait_recv()
        gather(t, 7).start()
        gather(t, 4).wait_recv()
        gather(t, 8).start()

    flip = lambda index: index + 1 - 2 * core
    owners = (tp, x_left, x_right, opposite, sib, flip(x_left), flip(x_right), flip(opposite))
    part_width = heads * HEAD_DIM

    def partial(t, sources):
        total = None
        for i in sources:
            at = pl.ds(pl.multiple_of(owners[i] * part_width, part_width), part_width)
            term = jnp.dot(gb[t, i], wo[at, :], preferred_element_type=F32)
            total = term if total is None else total + term
        return total

    def begin(t):
        for message in (2, 5, 6):
            gather(t, message).wait_recv()
        part[t] = partial(t, (0, 1, 2, 4, 5, 6))

    def project(t):
        for message in (7, 8):
            gather(t, message).wait_recv()
        out_ref[t * tile:(t + 1) * tile, :] = (part[t] + partial(t, (3, 7))).astype(BF16)

    wo_copy.wait()
    for t in range(TILES):
        unit(t, RX, False)
        finish(t)
    relay(0)
    relay(1)
    begin(0)
    relay(2)
    begin(1)
    relay(3)
    begin(2)
    across(0)
    begin(3)
    across(1)
    project(0)
    across(2)
    project(1)
    across(3)
    project(2)
    project(3)

    for t in range(TILES):
        for message in range(9):
            gather(t, message).wait_send()
    for condition, message, c, used in sent:
        @pl.when(condition)
        def _():
            halo(message, message, right, c, used).wait_send()


def shards(tokens, norm_gain, query_weight, key_weight, value_weight, out_weight, segments):
    rows, width = tokens.shape
    heads = query_weight.shape[1] // HEAD_DIM
    freqs = 10000.0 ** (-(jnp.arange(HEAD_DIM // 2, dtype=F32) * 2.0 / HEAD_DIM))
    freqs = jnp.concatenate([freqs, freqs])[None, :]
    tile = rows // TILES
    vmem = pl.BlockSpec(memory_space=pltpu.VMEM)
    hbm = pl.BlockSpec(memory_space=pl.ANY)
    return pl.pallas_call(
        kernel,
        out_shape=pltpu.VMEM((rows, out_weight.shape[1]), BF16),
        in_specs=[hbm, vmem, vmem, vmem, hbm, hbm, hbm, hbm],
        out_specs=vmem,
        scratch_shapes=[
            pltpu.VMEM((rows, width), BF16),
            pltpu.VMEM((rows, width), BF16),
            pltpu.VMEM(query_weight.shape, BF16),
            pltpu.VMEM((width, 2 * HEAD_DIM), BF16),
            pltpu.VMEM(out_weight.shape, BF16),
            pltpu.VMEM((9, rows, 2 * HEAD_DIM), BF16),
            pltpu.VMEM((TILES, heads * tile, HEAD_DIM), BF16),
            pltpu.VMEM((TILES, heads * tile, HEAD_DIM), F32),
            pltpu.VMEM((TILES, heads * tile, 2 * HEAD_DIM), F32),
            pltpu.VMEM((TILES, 8, tile, heads * HEAD_DIM), BF16),
            pltpu.VMEM((TILES, tile, out_weight.shape[1]), F32),
            pltpu.VMEM((rows, HEAD_DIM), F32),
            pltpu.VMEM((rows, HEAD_DIM), F32),
            pltpu.VMEM((rows, HEAD_DIM), jnp.int32),
            pltpu.SemaphoreType.DMA((TILES,)),
            pltpu.SemaphoreType.DMA((4,)),
            pltpu.SemaphoreType.DMA((11, TILES)),
            pltpu.SemaphoreType.DMA((9, TILES)),
            pltpu.SemaphoreType.DMA((TILES, 9)),
            pltpu.SemaphoreType.DMA((TILES, 9)),
        ],
        compiler_params=pltpu.CompilerParams(
            collective_id=0, has_side_effects=True, vmem_limit_bytes=56 << 20),
    )(tokens, norm_gain[None, :], freqs, segments.reshape(-1, HEAD_DIM),
      query_weight, key_weight, value_weight, out_weight)


def solution(mesh):
    return jax.shard_map(
        shards,
        mesh=mesh,
        in_specs=(
            P("seq", None),
            P(),
            P(None, "tp"),
            P(None, "tp"),
            P(None, "tp"),
            P(None, "tp"),
            P(),
        ),
        out_specs=P("seq", "tp"),
        check_vma=False,
    )
```

```python
import math

import jax
import jax.numpy as jnp
from jax import lax
from jax.experimental import pallas as pl
from jax.experimental.pallas import tpu as pltpu
from jax.sharding import PartitionSpec as P

HEAD_DIM = 128
WINDOW = 4096
TILES = 4
Z1, Z2, LA, L1, RA, R1, LX, RX = range(1, 9)
F32 = jnp.float32
BF16 = jnp.bfloat16


def pick(y, options):
    value = jnp.int32(options[3])
    for i in (2, 1, 0):
        value = jnp.where(y == i, jnp.int32(options[i]), value)
    return value


def kernel(tok_hbm, gain_ref, freq_ref, seg_ref, wq_hbm, wk_hbm, wv_hbm, wo_hbm, out_ref,
           xs, nrm, wq, wkv, wo, kv, qs, m_s, acc, gb, part, cos_s, sin_s, low_s,
           tok_sem, w_sem, ksend, krecv, gsend, grecv):
    rows, width = xs.shape
    heads = wq.shape[1] // HEAD_DIM
    tile = rows // TILES
    seq = lax.axis_index("seq")
    tp = lax.axis_index("tp")
    y = lax.rem(seq, 4)
    z = seq // 4
    z_last = lax.axis_size("seq") // 4 - 1
    row0 = z * 4
    z_next = lax.rem(seq + 4, 32)
    z_prev = lax.rem(seq + 28, 32)
    right = row0 + lax.rem(y + 1, 4)
    left = row0 + lax.rem(y + 3, 4)
    core = lax.rem(tp, 2)
    x_right = lax.rem(tp + 2, 8)
    x_left = lax.rem(tp + 6, 8)
    sib = tp + 1 - 2 * core
    opposite = lax.rem(tp + 4, 8)

    tok_copies = [
        pltpu.make_async_copy(tok_hbm.at[pl.ds(i * tile, tile)], xs.at[pl.ds(i * tile, tile)], tok_sem.at[i])
        for i in range(TILES)
    ]
    wk_copy = pltpu.make_async_copy(wk_hbm, wkv.at[:, pl.ds(0, HEAD_DIM)], w_sem.at[0])
    wv_copy = pltpu.make_async_copy(wv_hbm, wkv.at[:, pl.ds(HEAD_DIM, HEAD_DIM)], w_sem.at[1])
    wq_copy = pltpu.make_async_copy(wq_hbm, wq, w_sem.at[2])
    wo_copy = pltpu.make_async_copy(wo_hbm, wo, w_sem.at[3])
    for copy in tok_copies[:2] + [wk_copy, wv_copy] + tok_copies[2:] + [wq_copy, wo_copy]:
        copy.start()

    barrier = pltpu.get_barrier_semaphore()
    for where in ({"seq": z_next}, {"seq": z_prev}, {"seq": right}, {"seq": left},
                  {"tp": x_right}, {"tp": x_left}, {"tp": sib}):
        pl.semaphore_signal(barrier, inc=1, device_id=where, device_id_type=pl.DeviceIdType.MESH)

    def count_below(value):
        hits = (seg_ref[...] < value).astype(F32)
        return jnp.sum(jnp.sum(hits, axis=0, keepdims=True), axis=1, keepdims=True).astype(jnp.int32)

    second, third = count_below(1), count_below(2)

    def tables(c):
        small = tile // 2
        shape = (small, HEAD_DIM)
        lane = lax.broadcasted_iota(jnp.int32, shape, 1)
        row = lax.broadcasted_iota(jnp.int32, shape, 0) + (seq * rows + c * tile)
        front = lane < HEAD_DIM // 2
        angle = jnp.where(front, row, row + small).astype(F32) * freq_ref[...]
        cosine, sine = jnp.cos(angle), jnp.sin(angle)
        other_cosine, other_sine = (pltpu.roll(value, HEAD_DIM // 2, 1) for value in (cosine, sine))
        for i in range(2):
            at = pl.ds(c * tile + i * small, small)
            mine = front if i == 0 else ~front
            turned = jnp.where(mine, sine, other_sine)
            cos_s[at, :] = jnp.where(mine, cosine, other_cosine)
            sin_s[at, :] = jnp.where(front, -turned, turned)
            position = row + i * small
            begin = jnp.where(position < second, 0, jnp.where(position < third, second, third))
            low_s[at, :] = jnp.maximum(position - (WINDOW - 1), begin)

    back = [0, 1, 2, pick(y, (2, 0, 0, 0)), 1, pick(y, (2, 2, 2, 0)), 1,
            pick(y, (1, 1, 0, 0)), pick(y, (2, 2, 1, 1))]
    side = [0, 0, 0, -1, -1, 1, 1, -2, 2]
    starts = [((z - back[s]) * 4 + lax.rem(y + side[s] + 4, 4)) * rows for s in range(9)]

    @pl.when(z < back[RX])
    def _():
        kv[RX] = jnp.zeros(kv.shape[1:], BF16)

    def norm_rows(i, carry):
        at = pl.ds(pl.multiple_of(i * 16, 16), 16)
        x = xs[at, :].astype(F32)
        scale = lax.rsqrt(jnp.mean(x * x, axis=-1, keepdims=True) + 1e-05)
        nrm[at, :] = (x * scale * gain_ref[...]).astype(BF16)
        return carry

    def rotate(x, cosine, sine):
        return x * cosine + pltpu.roll(x, HEAD_DIM // 2, 1) * sine

    sent = []

    def halo(message, source, where, c, used=None):
        part = pl.ds(c * tile, tile)
        return pltpu.make_async_remote_copy(
            src_ref=kv.at[source, part], dst_ref=kv.at[message, part],
            send_sem=ksend.at[message if used is None else used, c], recv_sem=krecv.at[message, c],
            device_id={"seq": where}, device_id_type=pl.DeviceIdType.MESH)

    def send(condition, message, source, where, c, used=None):
        sent.append((condition, message, c, used))

        @pl.when(condition)
        def _():
            halo(message, source, where, c, used).start()

    def got(message, c, condition=None):
        valid = z >= back[message]

        @pl.when(valid if condition is None else valid & condition)
        def _():
            halo(message, message, right, c).wait_recv()

    inner = (y == 1) | (y == 2)
    outer = (y == 0) | (y == 3)
    below = (z >= 1) & (z < z_last)

    def from_z1(c):
        got(Z1, c)
        send(below, Z2, Z1, z_next, c)
        send(z >= 1, R1, Z1, left, c)
        send(z >= 1, L1, Z1, right, c)

    def from_z2(c):
        got(Z2, c)
        if c < TILES // 2:
            send((z >= 2) & (y >= 2), RA, Z2, left, c)
        send((z >= 2) & (y == 3), LA, Z2, right, c)

    def from_la(c):
        got(LA, c, inner)
        send(inner, LX, LA, right, c)

    def from_r1(c):
        got(R1, c)
        send(((y == 0) if c < TILES // 2 else (y < 3)) & below, RA, R1, z_next, c, 9)
        if c >= TILES // 2:
            send((y == 1) & (z >= 1), LX, R1, left, c, 10)

    def pass_r1(c):
        send(outer & (z >= 1), RX, R1, left, c)

    def from_l1(c, condition=True):
        got(L1, c, condition)
        relays = outer if c < TILES // 2 else y == 0
        send(condition & relays & (z >= 1), LX, L1, right, c)

    def from_ra(c, condition):
        got(RA, c, condition)
        send(condition & (z >= 2), RX, RA, left, c)

    tables(0)
    for chunks in ((0,), (1,), (2, 3)):
        for c in chunks:
            tok_copies[c].wait()
            lax.fori_loop(c * (tile // 16), (c + 1) * (tile // 16), norm_rows, 0, unroll=2)
            if c == 0:
                wk_copy.wait()
                wv_copy.wait()
            else:
                tables(c)
        at = pl.ds(chunks[0] * tile, len(chunks) * tile)
        both = jnp.dot(nrm[at, :], wkv[...], preferred_element_type=F32)
        kv[0, at, :HEAD_DIM] = rotate(both[:, :HEAD_DIM], cos_s[at, :], sin_s[at, :]).astype(BF16)
        kv[0, at, HEAD_DIM:] = both[:, HEAD_DIM:].astype(BF16)
        if chunks[0] == 0:
            pl.semaphore_wait(barrier, 7)
        for c in chunks:
            send(z < z_last, Z1, 0, z_next, c)
            send(y < 3, LA, 0, right, c)
            send(y == 0, RA, 0, left, c)

    wq_copy.wait()
    for pair in range(heads // 2):
        both = jnp.dot(nrm[...], wq[:, pair * 256:(pair + 1) * 256], preferred_element_type=F32)
        for j in range(2):
            h = pair * 2 + j
            q = rotate(both[:, j * 128:(j + 1) * 128], cos_s[...], sin_s[...]).astype(BF16)
            for t in range(TILES):
                qs[t, h * tile:(h + 1) * tile, :] = q[t * tile:(t + 1) * tile, :]
    from_z1(0)

    factor = math.log2(math.e) / math.sqrt(HEAD_DIM)
    lanes = lax.broadcasted_iota(jnp.int32, (tile, HEAD_DIM), 1)
    ones = jnp.ones((rows, HEAD_DIM), BF16)

    def start_of(slot):
        if isinstance(slot, int):
            return starts[slot]
        value = starts[8]
        for s in range(7, 0, -1):
            value = jnp.where(slot == s, starts[s], value)
        return value

    def unit(t, slot, first, piece=None):
        count = rows if piece is None else rows // 2
        at = slice(None) if piece is None else pl.ds(piece * count, count)
        k = kv[slot, at, :HEAD_DIM]
        v = jnp.concatenate([kv[slot, at, HEAD_DIM:], ones[:count]], axis=1)
        low = low_s[t * tile:(t + 1) * tile, :] - (start_of(slot) + (0 if piece is None else piece * count))
        s = lax.dot_general(qs[t], k, (((1,), (1,)), ((), ())), preferred_element_type=F32)
        chunks = []
        for c in range(count // 128):
            ok = lanes + c * 128 >= low
            if first:
                mine = lax.broadcasted_iota(jnp.int32, (tile, HEAD_DIM), 0) + t * tile
                ok = ok & (lanes + c * 128 <= mine)
            part = s[:, c * 128:(c + 1) * 128]
            chunks.append(jnp.concatenate(
                [jnp.where(ok, part[h * tile:(h + 1) * tile], F32(-1e30)) for h in range(heads)], axis=0))
        top = chunks[0]
        for part in chunks[1:]:
            top = jnp.maximum(top, part)
        peak = jnp.max(top, axis=1, keepdims=True) * factor
        peak = jnp.broadcast_to(peak, (heads * tile, HEAD_DIM))
        if not first:
            old = m_s[t]
            peak = jnp.maximum(old, peak)
        p = jnp.concatenate([jnp.exp2(part * factor - peak).astype(BF16) for part in chunks], axis=1)
        new = jnp.dot(p, v, preferred_element_type=F32)
        m_s[t] = peak
        if first:
            acc[t] = new
        else:
            decay = jnp.exp2(old - peak)
            acc[t, :, :HEAD_DIM] = acc[t, :, :HEAD_DIM] * decay + new[:, :HEAD_DIM]
            acc[t, :, HEAD_DIM:] = acc[t, :, HEAD_DIM:] * decay + new[:, HEAD_DIM:]

    def sweep(slot, first=False, piece=None, condition=True):
        @pl.when((start_of(slot) >= 0) & condition)
        def _():
            for t in range(TILES):
                unit(t, slot, first, piece)

    order = [pick(y, options) for options in zip(
        (Z1, R1, L1, Z2, LX, RA, LA), (Z1, LA, R1, Z2, L1, RA, LX),
        (Z1, LA, R1, Z2, L1, RA, LX), (Z1, LA, RA, R1, Z2, L1, LX))]

    def got_all(message, condition=None):
        for c in range(TILES):
            got(message, c, condition)

    sweep(0, True)
    from_z1(1)
    sweep(Z1, piece=0)
    from_z1(2)
    from_z1(3)
    for c in range(TILES):
        from_la(c)
    sweep(Z1, piece=1)
    from_z2(0)
    from_r1(0)
    from_r1(1)
    got_all(LA, y == 3)
    sweep(order[1], condition=y > 0)
    sweep(R1, piece=0, condition=y == 0)
    from_z2(1)
    from_l1(0)
    from_l1(1)
    sweep(L1, piece=0, condition=y == 0)
    from_r1(2)
    from_r1(3)
    for c in range(TILES):
        pass_r1(c)
    from_l1(2, y == 0)
    from_l1(3, y == 0)
    got_all(RA, y == 3)
    sweep(order[2], condition=y > 0)
    sweep(R1, piece=1, condition=y == 0)
    sweep(L1, piece=1, condition=y == 0)
    from_z2(2)
    from_l1(2, y > 0)
    from_z2(3)
    from_l1(3, y > 0)
    from_ra(0, inner)
    sweep(order[3])
    from_ra(1, inner)
    from_ra(2, inner)
    got_all(LX, y == 0)
    sweep(order[4])
    from_ra(3, inner)
    got_all(RA, y == 0)
    sweep(order[5])
    got_all(LX, y > 0)
    got_all(LA, y == 0)
    sweep(order[6])
    got_all(RX)

    half_tile = tile // 2
    upper, lower = pl.ds(0, half_tile), pl.ds(half_tile, half_tile)
    everything = pl.ds(0, tile)
    gather_plan = (
        (0, 1, everything, x_right), (0, 2, everything, x_left), (0, 4, everything, sib),
        (1, 3, upper, x_right), (2, 3, lower, x_left),
        (1, 5, everything, sib), (2, 6, everything, sib),
        (3, 7, upper, sib), (3, 7, lower, sib))

    def gather(t, message):
        source, target, part, where = gather_plan[message]
        return pltpu.make_async_remote_copy(
            src_ref=gb.at[t, source, part], dst_ref=gb.at[t, target, part],
            send_sem=gsend.at[t, message], recv_sem=grecv.at[t, message],
            device_id={"tp": where}, device_id_type=pl.DeviceIdType.MESH)

    def finish(t):
        result = (acc[t, :, :HEAD_DIM] / acc[t, :, HEAD_DIM:]).astype(BF16)
        for h in range(heads):
            gb[t, 0, :, h * 128:(h + 1) * 128] = result[h * tile:(h + 1) * tile]
        for message in (0, 1, 2):
            gather(t, message).start()

    def relay(t):
        gather(t, 0).wait_recv()
        gather(t, 3).start()
        gather(t, 5).start()
        gather(t, 1).wait_recv()
        gather(t, 4).start()
        gather(t, 6).start()

    def across(t):
        gather(t, 3).wait_recv()
        gather(t, 7).start()
        gather(t, 4).wait_recv()
        gather(t, 8).start()

    flip = lambda index: index + 1 - 2 * core
    owners = (tp, x_left, x_right, opposite, sib, flip(x_left), flip(x_right), flip(opposite))
    part_width = heads * HEAD_DIM

    def partial(t, sources):
        total = None
        for i in sources:
            at = pl.ds(pl.multiple_of(owners[i] * part_width, part_width), part_width)
            term = jnp.dot(gb[t, i], wo[at, :], preferred_element_type=F32)
            total = term if total is None else total + term
        return total

    def begin(t):
        for message in (2, 5, 6):
            gather(t, message).wait_recv()
        part[t] = partial(t, (0, 1, 2, 4, 5, 6))

    def project(t):
        for message in (7, 8):
            gather(t, message).wait_recv()
        out_ref[t * tile:(t + 1) * tile, :] = (part[t] + partial(t, (3, 7))).astype(BF16)

    wo_copy.wait()
    for t in range(TILES):
        unit(t, RX, False)
        finish(t)
    relay(0)
    relay(1)
    begin(0)
    relay(2)
    begin(1)
    relay(3)
    begin(2)
    across(0)
    begin(3)
    across(1)
    project(0)
    across(2)
    project(1)
    across(3)
    project(2)
    project(3)

    for t in range(TILES):
        for message in range(9):
            gather(t, message).wait_send()
    for condition, message, c, used in sent:
        @pl.when(condition)
        def _():
            halo(message, message, right, c, used).wait_send()


def shards(tokens, norm_gain, query_weight, key_weight, value_weight, out_weight, segments):
    rows, width = tokens.shape
    heads = query_weight.shape[1] // HEAD_DIM
    freqs = 10000.0 ** (-(jnp.arange(HEAD_DIM // 2, dtype=F32) * 2.0 / HEAD_DIM))
    freqs = jnp.concatenate([freqs, freqs])[None, :]
    tile = rows // TILES
    vmem = pl.BlockSpec(memory_space=pltpu.VMEM)
    hbm = pl.BlockSpec(memory_space=pl.ANY)
    return pl.pallas_call(
        kernel,
        out_shape=pltpu.VMEM((rows, out_weight.shape[1]), BF16),
        in_specs=[hbm, vmem, vmem, vmem, hbm, hbm, hbm, hbm],
        out_specs=vmem,
        scratch_shapes=[
            pltpu.VMEM((rows, width), BF16),
            pltpu.VMEM((rows, width), BF16),
            pltpu.VMEM(query_weight.shape, BF16),
            pltpu.VMEM((width, 2 * HEAD_DIM), BF16),
            pltpu.VMEM(out_weight.shape, BF16),
            pltpu.VMEM((9, rows, 2 * HEAD_DIM), BF16),
            pltpu.VMEM((TILES, heads * tile, HEAD_DIM), BF16),
            pltpu.VMEM((TILES, heads * tile, HEAD_DIM), F32),
            pltpu.VMEM((TILES, heads * tile, 2 * HEAD_DIM), F32),
            pltpu.VMEM((TILES, 8, tile, heads * HEAD_DIM), BF16),
            pltpu.VMEM((TILES, tile, out_weight.shape[1]), F32),
            pltpu.VMEM((rows, HEAD_DIM), F32),
            pltpu.VMEM((rows, HEAD_DIM), F32),
            pltpu.VMEM((rows, HEAD_DIM), jnp.int32),
            pltpu.SemaphoreType.DMA((TILES,)),
            pltpu.SemaphoreType.DMA((4,)),
            pltpu.SemaphoreType.DMA((11, TILES)),
            pltpu.SemaphoreType.DMA((9, TILES)),
            pltpu.SemaphoreType.DMA((TILES, 9)),
            pltpu.SemaphoreType.DMA((TILES, 9)),
        ],
        compiler_params=pltpu.CompilerParams(
            collective_id=0, has_side_effects=True, vmem_limit_bytes=56 << 20),
    )(tokens, norm_gain[None, :], freqs, segments.reshape(-1, HEAD_DIM),
      query_weight, key_weight, value_weight, out_weight)


def solution(mesh):
    return jax.shard_map(
        shards,
        mesh=mesh,
        in_specs=(
            P("seq", None),
            P(),
            P(None, "tp"),
            P(None, "tp"),
            P(None, "tp"),
            P(None, "tp"),
            P(),
        ),
        out_specs=P("seq", "tp"),
        check_vma=False,
    )
```

```python
import math

import jax
import jax.numpy as jnp
from jax import lax
from jax.experimental import pallas as pl
from jax.experimental.pallas import tpu as pltpu
from jax.sharding import PartitionSpec as P

HEAD_DIM = 128
WINDOW = 4096
TILES = 4
Z1, Z2, LA, L1, RA, R1, LX, RX = range(1, 9)
F32 = jnp.float32
BF16 = jnp.bfloat16


def pick(y, options):
    value = jnp.int32(options[3])
    for i in (2, 1, 0):
        value = jnp.where(y == i, jnp.int32(options[i]), value)
    return value


def kernel(tok_hbm, gain_ref, freq_ref, seg_ref, wq_hbm, wk_hbm, wv_hbm, wo_hbm, out_ref,
           xs, nrm, wq, wkv, wo, kv, qs, m_s, acc, gb, part, cos_s, sin_s, low_s,
           tok_sem, w_sem, ksend, krecv, gsend, grecv):
    rows, width = xs.shape
    heads = wq.shape[1] // HEAD_DIM
    tile = rows // TILES
    seq = lax.axis_index("seq")
    tp = lax.axis_index("tp")
    y = lax.rem(seq, 4)
    z = seq // 4
    z_last = lax.axis_size("seq") // 4 - 1
    row0 = z * 4
    z_next = lax.rem(seq + 4, 32)
    z_prev = lax.rem(seq + 28, 32)
    right = row0 + lax.rem(y + 1, 4)
    left = row0 + lax.rem(y + 3, 4)
    core = lax.rem(tp, 2)
    x_right = lax.rem(tp + 2, 8)
    x_left = lax.rem(tp + 6, 8)
    sib = tp + 1 - 2 * core
    opposite = lax.rem(tp + 4, 8)

    tok_copies = [
        pltpu.make_async_copy(tok_hbm.at[pl.ds(i * tile, tile)], xs.at[pl.ds(i * tile, tile)], tok_sem.at[i])
        for i in range(TILES)
    ]
    wk_copy = pltpu.make_async_copy(wk_hbm, wkv.at[:, pl.ds(0, HEAD_DIM)], w_sem.at[0])
    wv_copy = pltpu.make_async_copy(wv_hbm, wkv.at[:, pl.ds(HEAD_DIM, HEAD_DIM)], w_sem.at[1])
    wq_copy = pltpu.make_async_copy(wq_hbm, wq, w_sem.at[2])
    wo_copy = pltpu.make_async_copy(wo_hbm, wo, w_sem.at[3])
    for copy in tok_copies[:2] + [wk_copy, wv_copy] + tok_copies[2:] + [wq_copy, wo_copy]:
        copy.start()

    barrier = pltpu.get_barrier_semaphore()
    for where in ({"seq": z_next}, {"seq": z_prev}, {"seq": right}, {"seq": left},
                  {"tp": x_right}, {"tp": x_left}, {"tp": sib}):
        pl.semaphore_signal(barrier, inc=1, device_id=where, device_id_type=pl.DeviceIdType.MESH)

    def count_below(value):
        hits = (seg_ref[...] < value).astype(F32)
        return jnp.sum(jnp.sum(hits, axis=0, keepdims=True), axis=1, keepdims=True).astype(jnp.int32)

    second, third = count_below(1), count_below(2)

    def tables(c):
        small = tile // 2
        shape = (small, HEAD_DIM)
        lane = lax.broadcasted_iota(jnp.int32, shape, 1)
        row = lax.broadcasted_iota(jnp.int32, shape, 0) + (seq * rows + c * tile)
        front = lane < HEAD_DIM // 2
        angle = jnp.where(front, row, row + small).astype(F32) * freq_ref[...]
        cosine, sine = jnp.cos(angle), jnp.sin(angle)
        other_cosine, other_sine = (pltpu.roll(value, HEAD_DIM // 2, 1) for value in (cosine, sine))
        for i in range(2):
            at = pl.ds(c * tile + i * small, small)
            mine = front if i == 0 else ~front
            turned = jnp.where(mine, sine, other_sine)
            cos_s[at, :] = jnp.where(mine, cosine, other_cosine)
            sin_s[at, :] = jnp.where(front, -turned, turned)
            position = row + i * small
            begin = jnp.where(position < second, 0, jnp.where(position < third, second, third))
            low_s[at, :] = jnp.maximum(position - (WINDOW - 1), begin)

    back = [0, 1, 2, pick(y, (2, 0, 0, 0)), 1, pick(y, (2, 2, 2, 0)), 1,
            pick(y, (1, 1, 0, 0)), pick(y, (2, 2, 1, 1))]
    side = [0, 0, 0, -1, -1, 1, 1, -2, 2]
    starts = [((z - back[s]) * 4 + lax.rem(y + side[s] + 4, 4)) * rows for s in range(9)]

    @pl.when(z < back[RX])
    def _():
        kv[RX] = jnp.zeros(kv.shape[1:], BF16)

    def norm_rows(i, carry):
        at = pl.ds(pl.multiple_of(i * 16, 16), 16)
        x = xs[at, :].astype(F32)
        scale = lax.rsqrt(jnp.mean(x * x, axis=-1, keepdims=True) + 1e-05)
        nrm[at, :] = (x * scale * gain_ref[...]).astype(BF16)
        return carry

    def rotate(x, cosine, sine):
        return x * cosine + pltpu.roll(x, HEAD_DIM // 2, 1) * sine

    sent = []

    def halo(message, source, where, c, used=None):
        part = pl.ds(c * tile, tile)
        return pltpu.make_async_remote_copy(
            src_ref=kv.at[source, part], dst_ref=kv.at[message, part],
            send_sem=ksend.at[message if used is None else used, c], recv_sem=krecv.at[message, c],
            device_id={"seq": where}, device_id_type=pl.DeviceIdType.MESH)

    def send(condition, message, source, where, c, used=None):
        sent.append((condition, message, c, used))

        @pl.when(condition)
        def _():
            halo(message, source, where, c, used).start()

    def got(message, c, condition=None):
        valid = z >= back[message]

        @pl.when(valid if condition is None else valid & condition)
        def _():
            halo(message, message, right, c).wait_recv()

    inner = (y == 1) | (y == 2)
    outer = (y == 0) | (y == 3)
    below = (z >= 1) & (z < z_last)

    def from_z1(c):
        got(Z1, c)
        send(below, Z2, Z1, z_next, c)
        send(z >= 1, R1, Z1, left, c)
        send(z >= 1, L1, Z1, right, c)

    def from_z2(c):
        got(Z2, c)
        if c < TILES // 2:
            send((z >= 2) & (y >= 2), RA, Z2, left, c)
        send((z >= 2) & (y == 3), LA, Z2, right, c)

    def from_la(c):
        got(LA, c, inner)
        send(inner, LX, LA, right, c)

    def from_r1(c):
        got(R1, c)
        send(((y == 0) if c < TILES // 2 else (y < 3)) & below, RA, R1, z_next, c, 9)
        if c >= TILES // 2:
            send((y == 1) & (z >= 1), LX, R1, left, c, 10)

    def pass_r1(c):
        send(outer & (z >= 1), RX, R1, left, c)

    def from_l1(c, condition=True):
        got(L1, c, condition)
        relays = outer if c < TILES // 2 else y == 0
        send(condition & relays & (z >= 1), LX, L1, right, c)

    def from_ra(c, condition):
        got(RA, c, condition)
        send(condition & (z >= 2), RX, RA, left, c)

    tables(0)
    for chunks in ((0,), (1,), (2, 3)):
        for c in chunks:
            tok_copies[c].wait()
            lax.fori_loop(c * (tile // 16), (c + 1) * (tile // 16), norm_rows, 0, unroll=2)
            if c == 0:
                wk_copy.wait()
                wv_copy.wait()
            else:
                tables(c)
        at = pl.ds(chunks[0] * tile, len(chunks) * tile)
        both = jnp.dot(nrm[at, :], wkv[...], preferred_element_type=F32)
        kv[0, at, :HEAD_DIM] = rotate(both[:, :HEAD_DIM], cos_s[at, :], sin_s[at, :]).astype(BF16)
        kv[0, at, HEAD_DIM:] = both[:, HEAD_DIM:].astype(BF16)
        if chunks[0] == 0:
            pl.semaphore_wait(barrier, 7)
        for c in chunks:
            send(z < z_last, Z1, 0, z_next, c)
            send(y < 3, LA, 0, right, c)
            send(y == 0, RA, 0, left, c)

    wq_copy.wait()
    for pair in range(heads // 2):
        both = jnp.dot(nrm[...], wq[:, pair * 256:(pair + 1) * 256], preferred_element_type=F32)
        for j in range(2):
            h = pair * 2 + j
            q = rotate(both[:, j * 128:(j + 1) * 128], cos_s[...], sin_s[...]).astype(BF16)
            for t in range(TILES):
                qs[t, h * tile:(h + 1) * tile, :] = q[t * tile:(t + 1) * tile, :]
    from_z1(0)

    factor = math.log2(math.e) / math.sqrt(HEAD_DIM)
    lanes = lax.broadcasted_iota(jnp.int32, (tile, HEAD_DIM), 1)
    ones = jnp.ones((rows, HEAD_DIM), BF16)

    def start_of(slot):
        if isinstance(slot, int):
            return starts[slot]
        value = starts[8]
        for s in range(7, 0, -1):
            value = jnp.where(slot == s, starts[s], value)
        return value

    def unit(t, slot, first, piece=None):
        count = rows if piece is None else rows // 2
        at = slice(None) if piece is None else pl.ds(piece * count, count)
        k = kv[slot, at, :HEAD_DIM]
        v = jnp.concatenate([kv[slot, at, HEAD_DIM:], ones[:count]], axis=1)
        low = low_s[t * tile:(t + 1) * tile, :] - (start_of(slot) + (0 if piece is None else piece * count))
        s = lax.dot_general(qs[t], k, (((1,), (1,)), ((), ())), preferred_element_type=F32)
        chunks = []
        for c in range(count // 128):
            ok = lanes + c * 128 >= low
            if first:
                mine = lax.broadcasted_iota(jnp.int32, (tile, HEAD_DIM), 0) + t * tile
                ok = ok & (lanes + c * 128 <= mine)
            part = s[:, c * 128:(c + 1) * 128]
            chunks.append(jnp.concatenate(
                [jnp.where(ok, part[h * tile:(h + 1) * tile], F32(-1e30)) for h in range(heads)], axis=0))
        top = chunks[0]
        for part in chunks[1:]:
            top = jnp.maximum(top, part)
        peak = jnp.max(top, axis=1, keepdims=True) * factor
        peak = jnp.broadcast_to(peak, (heads * tile, HEAD_DIM))
        if not first:
            old = m_s[t]
            peak = jnp.maximum(old, peak)
        p = jnp.concatenate([jnp.exp2(part * factor - peak).astype(BF16) for part in chunks], axis=1)
        new = jnp.dot(p, v, preferred_element_type=F32)
        m_s[t] = peak
        if first:
            acc[t] = new
        else:
            decay = jnp.exp2(old - peak)
            acc[t, :, :HEAD_DIM] = acc[t, :, :HEAD_DIM] * decay + new[:, :HEAD_DIM]
            acc[t, :, HEAD_DIM:] = acc[t, :, HEAD_DIM:] * decay + new[:, HEAD_DIM:]

    def sweep(slot, first=False, piece=None, condition=True):
        @pl.when((start_of(slot) >= 0) & condition)
        def _():
            for t in range(TILES):
                unit(t, slot, first, piece)

    order = [pick(y, options) for options in zip(
        (Z1, R1, L1, Z2, LX, RA, LA), (Z1, LA, R1, Z2, L1, RA, LX),
        (Z1, LA, R1, Z2, L1, RA, LX), (Z1, LA, RA, R1, Z2, L1, LX))]

    def got_all(message, condition=None):
        for c in range(TILES):
            got(message, c, condition)

    sweep(0, True)
    from_z1(1)
    sweep(Z1, piece=0)
    from_z1(2)
    from_z1(3)
    for c in range(TILES):
        from_la(c)
    sweep(Z1, piece=1)
    from_z2(0)
    from_r1(0)
    from_r1(1)
    from_l1(0)
    got_all(LA, y == 3)
    sweep(order[1], condition=y > 0)
    sweep(R1, piece=0, condition=y == 0)
    from_l1(1)
    from_z2(1)
    sweep(L1, piece=0, condition=y == 0)
    from_r1(2)
    from_r1(3)
    for c in range(TILES):
        pass_r1(c)
    from_l1(2, y == 0)
    from_l1(3, y == 0)
    got_all(RA, y == 3)
    sweep(order[2], condition=y > 0)

    @pl.when((start_of(R1) >= 0) & (y == 0))
    def _():
        for t in range(TILES):
            unit(t, R1, False, 1)
            unit(t, L1, False, 1)

    from_z2(2)
    from_l1(2, y > 0)
    from_z2(3)
    from_l1(3, y > 0)
    from_ra(0, inner)
    sweep(order[3])
    from_ra(1, inner)
    from_ra(2, inner)
    got_all(LX, y == 0)
    sweep(order[4])
    from_ra(3, inner)
    got_all(RA, y == 0)
    sweep(order[5])
    got_all(LX, y > 0)
    got_all(LA, y == 0)
    sweep(order[6])
    got_all(RX)

    half_tile = tile // 2
    upper, lower = pl.ds(0, half_tile), pl.ds(half_tile, half_tile)
    everything = pl.ds(0, tile)
    gather_plan = (
        (0, 1, everything, x_right), (0, 2, everything, x_left), (0, 4, everything, sib),
        (1, 3, upper, x_right), (2, 3, lower, x_left),
        (1, 5, everything, sib), (2, 6, everything, sib),
        (3, 7, upper, sib), (3, 7, lower, sib))

    def gather(t, message):
        source, target, part, where = gather_plan[message]
        return pltpu.make_async_remote_copy(
            src_ref=gb.at[t, source, part], dst_ref=gb.at[t, target, part],
            send_sem=gsend.at[t, message], recv_sem=grecv.at[t, message],
            device_id={"tp": where}, device_id_type=pl.DeviceIdType.MESH)

    def finish(t):
        result = (acc[t, :, :HEAD_DIM] / acc[t, :, HEAD_DIM:]).astype(BF16)
        for h in range(heads):
            gb[t, 0, :, h * 128:(h + 1) * 128] = result[h * tile:(h + 1) * tile]
        for message in (0, 1, 2):
            gather(t, message).start()

    def relay(t):
        gather(t, 0).wait_recv()
        gather(t, 3).start()
        gather(t, 5).start()
        gather(t, 1).wait_recv()
        gather(t, 4).start()
        gather(t, 6).start()

    def across(t):
        gather(t, 3).wait_recv()
        gather(t, 7).start()
        gather(t, 4).wait_recv()
        gather(t, 8).start()

    flip = lambda index: index + 1 - 2 * core
    owners = (tp, x_left, x_right, opposite, sib, flip(x_left), flip(x_right), flip(opposite))
    part_width = heads * HEAD_DIM

    def partial(t, sources):
        total = None
        for i in sources:
            at = pl.ds(pl.multiple_of(owners[i] * part_width, part_width), part_width)
            term = jnp.dot(gb[t, i], wo[at, :], preferred_element_type=F32)
            total = term if total is None else total + term
        return total

    def begin(t):
        for message in (2, 5, 6):
            gather(t, message).wait_recv()
        part[t] = partial(t, (0, 1, 2, 4, 5, 6))

    def project(t):
        for message in (7, 8):
            gather(t, message).wait_recv()
        out_ref[t * tile:(t + 1) * tile, :] = (part[t] + partial(t, (3, 7))).astype(BF16)

    wo_copy.wait()
    for t in range(TILES):
        unit(t, RX, False)
        finish(t)
    relay(0)
    relay(1)
    begin(0)
    relay(2)
    begin(1)
    relay(3)
    begin(2)
    across(0)
    begin(3)
    across(1)
    project(0)
    across(2)
    project(1)
    across(3)
    project(2)
    project(3)

    for t in range(TILES):
        for message in range(9):
            gather(t, message).wait_send()
    for condition, message, c, used in sent:
        @pl.when(condition)
        def _():
            halo(message, message, right, c, used).wait_send()


def shards(tokens, norm_gain, query_weight, key_weight, value_weight, out_weight, segments):
    rows, width = tokens.shape
    heads = query_weight.shape[1] // HEAD_DIM
    freqs = 10000.0 ** (-(jnp.arange(HEAD_DIM // 2, dtype=F32) * 2.0 / HEAD_DIM))
    freqs = jnp.concatenate([freqs, freqs])[None, :]
    tile = rows // TILES
    vmem = pl.BlockSpec(memory_space=pltpu.VMEM)
    hbm = pl.BlockSpec(memory_space=pl.ANY)
    return pl.pallas_call(
        kernel,
        out_shape=pltpu.VMEM((rows, out_weight.shape[1]), BF16),
        in_specs=[hbm, vmem, vmem, vmem, hbm, hbm, hbm, hbm],
        out_specs=vmem,
        scratch_shapes=[
            pltpu.VMEM((rows, width), BF16),
            pltpu.VMEM((rows, width), BF16),
            pltpu.VMEM(query_weight.shape, BF16),
            pltpu.VMEM((width, 2 * HEAD_DIM), BF16),
            pltpu.VMEM(out_weight.shape, BF16),
            pltpu.VMEM((9, rows, 2 * HEAD_DIM), BF16),
            pltpu.VMEM((TILES, heads * tile, HEAD_DIM), BF16),
            pltpu.VMEM((TILES, heads * tile, HEAD_DIM), F32),
            pltpu.VMEM((TILES, heads * tile, 2 * HEAD_DIM), F32),
            pltpu.VMEM((TILES, 8, tile, heads * HEAD_DIM), BF16),
            pltpu.VMEM((TILES, tile, out_weight.shape[1]), F32),
            pltpu.VMEM((rows, HEAD_DIM), F32),
            pltpu.VMEM((rows, HEAD_DIM), F32),
            pltpu.VMEM((rows, HEAD_DIM), jnp.int32),
            pltpu.SemaphoreType.DMA((TILES,)),
            pltpu.SemaphoreType.DMA((4,)),
            pltpu.SemaphoreType.DMA((11, TILES)),
            pltpu.SemaphoreType.DMA((9, TILES)),
            pltpu.SemaphoreType.DMA((TILES, 9)),
            pltpu.SemaphoreType.DMA((TILES, 9)),
        ],
        compiler_params=pltpu.CompilerParams(
            collective_id=0, has_side_effects=True, vmem_limit_bytes=56 << 20),
    )(tokens, norm_gain[None, :], freqs, segments.reshape(-1, HEAD_DIM),
      query_weight, key_weight, value_weight, out_weight)


def solution(mesh):
    return jax.shard_map(
        shards,
        mesh=mesh,
        in_specs=(
            P("seq", None),
            P(),
            P(None, "tp"),
            P(None, "tp"),
            P(None, "tp"),
            P(None, "tp"),
            P(),
        ),
        out_specs=P("seq", "tp"),
        check_vma=False,
    )
```
